256 devices in a mesh: gx: 16 (over x, y), gy: 16 (over z, core).
Axes of the slice: x: 4, y: 4, z: 8, core: 2. Of those that a mesh axis runs over, the one named last changes fastest.
Arguments:
- initial_value: float32 [64, 128, 1024], P('gx', 'gy'), may hold values from -3.5 to 3.5
- disturbance: float32 [64, 128], P('gx', 'gy'), may hold values from 0.05 to 4.4
Outputs:
- final_value: float32 [64, 128, 1024], P('gx', 'gy')
The draws below stay inside these ranges and needn't reach their ends.
All inputs are finite; a program needn't handle non-finite values.
Results may differ from the reference program's by a relative error of at most 0.00002.
Values sent between devices are 32-bit elements; how exact they have to be, the bound alone decides.
A program may use at most 64 MiB of HBM per device.

```python
import math
import jax
import jax.numpy as jnp
from jax import lax

HEADINGS = 16
SPEEDS = 16
TURNS = 4
LANES = 1024
NX = 64
NY = 128


def draw_initial_value(key, part):
    grid_x = ((jnp.arange(NX, dtype=jnp.int32).astype(jnp.float32) - NX / 2.0 + 0.5) * 0.1)[:, None, None]
    grid_y = ((jnp.arange(NY, dtype=jnp.int32).astype(jnp.float32) - NY / 2.0 + 0.5) * 0.1)[None, :, None]
    lanes_all = jnp.arange(LANES, dtype=jnp.int32)
    heading = -math.pi + ((lanes_all % HEADINGS).astype(jnp.float32) + 0.5) * (2.0 * math.pi / HEADINGS)
    speed = 1.0 + 0.1 * (lanes_all // HEADINGS % SPEEDS).astype(jnp.float32)
    turning = 0.1 * ((lanes_all // (HEADINGS * SPEEDS)).astype(jnp.float32) - (TURNS - 1) / 2.0)
    smooth = jnp.sin(0.3 * grid_x) * jnp.cos(0.2 * grid_y) + (0.4 * jnp.cos(heading - 0.5) + 0.3 * speed + 0.8 * turning)[None, None, :]
    noise = 0.2 * jnp.clip(jax.random.normal(key, (NX, NY, LANES), jnp.float32), -4.0, 4.0)
    return jnp.clip(smooth + noise, -3.5, 3.5)


def draw_disturbance(key, part):
    rows = jnp.arange(NX, dtype=jnp.int32).astype(jnp.float32)
    columns = jnp.arange(NY, dtype=jnp.int32).astype(jnp.float32)
    rows_rise = 1.0 + 2.0 * rows / (NX - 1)
    columns_rise = 1.0 + 2.0 * columns / (NY - 1)
    trend = 0.15 * rows_rise[:, None] * columns_rise[None, :]
    centre_rows = jax.random.uniform(jax.random.fold_in(key, 11), (), jnp.float32, 0.0, NX - 1.0)
    centre_columns = jax.random.uniform(jax.random.fold_in(key, 12), (), jnp.float32, 0.0, NY - 1.0)
    spread = jax.random.uniform(jax.random.fold_in(key, 13), (), jnp.float32, 5.0, 15.0)
    height = jax.random.uniform(jax.random.fold_in(key, 14), (), jnp.float32, 1.0, 3.0)
    distance = (rows[:, None] - centre_rows) ** 2 + (columns[None, :] - centre_columns) ** 2
    gust = height * jnp.exp(-distance / (2.0 * spread * spread))
    rough_key = jax.random.fold_in(key, 15)
    rough = jnp.exp(jax.random.uniform(rough_key, (NX, NY), jnp.float32, math.log(0.5), 0.0))
    return (trend + gust) * rough


def setup_inputs(seed: int = 0) -> dict:
    key_of = jax.random.split(jax.random.key(seed), 3)
    initial_value = draw_initial_value(jax.random.fold_in(key_of[2], 71), 0)
    disturbance = draw_disturbance(jax.random.fold_in(key_of[2], 71), 0)
    return {"initial_value": initial_value, "disturbance": disturbance}


step_xy = 0.1
step_speed = 0.1
step_turn = 0.1
speed_low = 1.0
accel = 0.5
torque = 0.3
courant = 0.75
smooth_eps = 1e-06
radius_eps = 0.01

def ghosts(grid_values, along):
    width = grid_values.shape[along]
    first = lax.slice_in_dim(grid_values, 0, 1, axis=along)
    second = lax.slice_in_dim(grid_values, 1, 2, axis=along)
    last_row = lax.slice_in_dim(grid_values, width - 1, width, axis=along)
    before_last = lax.slice_in_dim(grid_values, width - 2, width - 1, axis=along)
    left_side = [first + factor * (first - second) for factor in (3.0, 2.0, 1.0)]
    right_side = [last_row + factor * (last_row - before_last) for factor in (1.0, 2.0, 3.0)]
    return jnp.concatenate(left_side + [grid_values] + right_side, axis=along)

def axis_shifts(extended, along, length_out):
    return [lax.slice_in_dim(extended, 3 + offset, 3 + offset + length_out, axis=along) for offset in range(-3, 4)]

def flat_shifts(grid_values, stride, extent, periodic):
    lanes_here = grid_values.shape[-1]
    position = jnp.arange(lanes_here, dtype=jnp.int32) // stride % extent

    def rolled(offset):
        return jnp.roll(grid_values, -offset * stride, axis=-1)
    result = []
    for offset in range(-3, 4):
        target = position + offset
        shifted = rolled(offset)
        if offset != 0:
            if periodic:
                wrapped = rolled(offset - extent if offset > 0 else offset + extent)
                shifted = jnp.where((target >= 0) & (target < extent), shifted, wrapped)
            else:
                for beyond in range(1, abs(offset) + 1):
                    if offset > 0:
                        edge_cell = rolled(offset - beyond)
                        inner_cell = rolled(offset - beyond - 1)
                        struck = target == extent - 1 + beyond
                    else:
                        edge_cell = rolled(offset + beyond)
                        inner_cell = rolled(offset + beyond + 1)
                        struck = target == -beyond
                    shifted = jnp.where(struck, edge_cell + beyond * (edge_cell - inner_cell), shifted)
        result.append(shifted)
    return result

def weno_side(slope_a, slope_b, slope_c, slope_d, slope_e):
    guess_one = slope_a / 3.0 - 7.0 * slope_b / 6.0 + 11.0 * slope_c / 6.0
    guess_two = -slope_b / 6.0 + 5.0 * slope_c / 6.0 + slope_d / 3.0
    guess_three = slope_c / 3.0 + 5.0 * slope_d / 6.0 - slope_e / 6.0
    rough_one = 13.0 / 12.0 * (slope_a - 2.0 * slope_b + slope_c) ** 2 + 0.25 * (slope_a - 4.0 * slope_b + 3.0 * slope_c) ** 2
    rough_two = 13.0 / 12.0 * (slope_b - 2.0 * slope_c + slope_d) ** 2 + 0.25 * (slope_b - slope_d) ** 2
    rough_three = 13.0 / 12.0 * (slope_c - 2.0 * slope_d + slope_e) ** 2 + 0.25 * (3.0 * slope_c - 4.0 * slope_d + slope_e) ** 2
    weight_one = 0.1 / (rough_one + smooth_eps) ** 2
    weight_two = 0.6 / (rough_two + smooth_eps) ** 2
    weight_three = 0.3 / (rough_three + smooth_eps) ** 2
    return (weight_one * guess_one + weight_two * guess_two + weight_three * guess_three) / (weight_one + weight_two + weight_three)

def weno(shifted, spacing):
    differ = [(shifted[offset + 1] - shifted[offset]) / spacing for offset in range(6)]
    left_slope = weno_side(differ[0], differ[1], differ[2], differ[3], differ[4])
    right_slope = weno_side(differ[5], differ[4], differ[3], differ[2], differ[1])
    return (left_slope, right_slope)

def flat_slopes(grid_values):
    return [weno(flat_shifts(grid_values, 1, HEADINGS, True), 2.0 * math.pi / HEADINGS), weno(flat_shifts(grid_values, HEADINGS, SPEEDS, False), step_speed), weno(flat_shifts(grid_values, HEADINGS * SPEEDS, TURNS, False), step_turn)]

def lane_coords():
    lanes_all = jnp.arange(LANES, dtype=jnp.int32)
    heading = -math.pi + ((lanes_all % HEADINGS).astype(jnp.float32) + 0.5) * (2.0 * math.pi / HEADINGS)
    speed = speed_low + step_speed * (lanes_all // HEADINGS % SPEEDS).astype(jnp.float32)
    turning = step_turn * ((lanes_all // (HEADINGS * SPEEDS)).astype(jnp.float32) - (TURNS - 1) / 2.0)
    return (speed * jnp.cos(heading), speed * jnp.sin(heading), turning)

def centered(slopes):
    return [(one_sided[0] + one_sided[1]) * 0.5 for one_sided in slopes]

def speed_bounds(means, disturb_cells, coords):
    radius = jnp.sqrt(means[0] * means[0] + means[1] * means[1] + radius_eps)
    bound_x = jnp.abs(coords[0] - disturb_cells * means[0] / radius)
    bound_y = jnp.abs(coords[1] - disturb_cells * means[1] / radius)
    return (bound_x, bound_y)

def change_rate(slopes, means, disturb_cells, coords, alpha_x, alpha_y):
    radius = jnp.sqrt(means[0] * means[0] + means[1] * means[1] + radius_eps)
    hamilton = means[0] * coords[0] + means[1] * coords[1] + means[2] * coords[2]
    hamilton = hamilton + accel * jnp.abs(means[3]) + torque * jnp.abs(means[4]) - disturb_cells * radius
    turn_peak = step_turn * (TURNS - 1) / 2.0
    for coefficient, one_sided in zip((alpha_x, alpha_y, turn_peak, accel, torque), slopes):
        hamilton = hamilton - coefficient * (one_sided[1] - one_sided[0]) * 0.5
    return -hamilton

def time_step(alpha_x, alpha_y):
    turn_peak = step_turn * (TURNS - 1) / 2.0
    total = alpha_x / step_xy + alpha_y / step_xy + turn_peak / (2.0 * math.pi / HEADINGS)
    return courant / (total + accel / step_speed + torque / step_turn)

def slopes_whole(grid_values):
    along_rows = axis_shifts(ghosts(grid_values, 0), 0, grid_values.shape[0])
    along_columns = axis_shifts(ghosts(grid_values, 1), 1, grid_values.shape[1])
    return [weno(along_rows, step_xy), weno(along_columns, step_xy)] + flat_slopes(grid_values)

def reference(initial_value, disturbance):
    coords = lane_coords()
    disturb_cells = disturbance[:, :, None]
    current = initial_value
    slopes = slopes_whole(current)
    means = centered(slopes)
    bound_x, bound_y = speed_bounds(means, disturb_cells, coords)
    alpha_x = jnp.max(bound_x)
    alpha_y = jnp.max(bound_y)
    for sweep_index in range(2):
        time_delta = time_step(alpha_x, alpha_y)
        if sweep_index > 0:
            slopes = slopes_whole(current)
            means = centered(slopes)
        first_section = current + time_delta * change_rate(slopes, means, disturb_cells, coords, alpha_x, alpha_y)
        slopes = slopes_whole(first_section)
        means = centered(slopes)
        if sweep_index == 0:
            peaks_two = speed_bounds(means, disturb_cells, coords)
        second_section = 0.75 * current + 0.25 * (first_section + time_delta * change_rate(slopes, means, disturb_cells, coords, alpha_x, alpha_y))
        slopes = slopes_whole(second_section)
        means = centered(slopes)
        if sweep_index == 0:
            peaks_three = speed_bounds(means, disturb_cells, coords)
        next_value = current / 3.0 + 2.0 / 3.0 * (second_section + time_delta * change_rate(slopes, means, disturb_cells, coords, alpha_x, alpha_y))
        if sweep_index == 0:
            alpha_x = jnp.maximum(jnp.max(peaks_two[0]), jnp.max(peaks_three[0]))
            alpha_y = jnp.maximum(jnp.max(peaks_two[1]), jnp.max(peaks_three[1]))
        current = next_value
    return current
```

```python
import functools
import math

import jax
import jax.numpy as jnp
import numpy as np
from jax import lax
from jax.experimental import pallas as pl
from jax.experimental.pallas import tpu as pltpu
from jax.sharding import PartitionSpec as P

HEADINGS = 16
SPEEDS = 16
TURNS = 4
LANES = HEADINGS * SPEEDS * TURNS

NX = 4
NY = 8
SUB = 8
LANE = 128
TILES = LANES // LANE
FX = NX + 6
FY = NY + 6

SCALE = 4.0
step_xy = 0.1
step_heading = 2.0 * math.pi / HEADINGS
accel = 0.5
torque = 0.3
turn_peak = 0.1 * (TURNS - 1) / 2.0
EPS_XY = 0.75e-6 * (SCALE * step_xy) ** 2
EPS_HEADING = 0.75e-6 * (SCALE * step_heading) ** 2
RADIUS = 0.01 * (SCALE * 12.0 * step_xy) ** 2

MESH = pl.DeviceIdType.MESH


def coordinate_tables():
    lanes = np.arange(LANES)
    heading = (-math.pi + ((lanes % HEADINGS) + 0.5) * step_heading).astype(np.float32)
    speed = (1.0 + 0.1 * (lanes // HEADINGS % SPEEDS)).astype(np.float32)
    vx = speed * np.cos(heading)
    vy = speed * np.sin(heading)
    return np.stack([vx, vy]).astype(np.float32).reshape(2, SUB, LANE)


def corrections(s1, s2, s3, x1, x2):
    a = s2 * s3
    b = s1 * s3
    c = s1 * s2
    r1 = a * a
    r2 = b * b
    r3 = c * c
    mid = r1 + r3 + 6.0 * r2
    den_right = mid + (r3 + r3)
    den_left = mid + (r1 + r1)
    y1 = r1 * x1
    y2 = r3 * x2
    both = y1 + y2
    both = both + both
    right = (both + y2) / den_right
    left = (both + y1) / den_left
    return right, left


def smooth_outer(inner, outer_sq, inner_sq, product):
    return (2.5 * inner_sq - 2.75 * product) + outer_sq


def line_slopes(cells, eps):
    n = len(cells) - 6
    diff = [b - a for a, b in zip(cells[:-1], cells[1:])]
    second = [b - a for a, b in zip(diff[:-1], diff[1:])]
    third = [b - a for a, b in zip(second[:-1], second[1:])]
    fourth = [b - a for a, b in zip(third[:-1], third[1:])]
    sq = [e * e for e in second]
    sq_eps = [q + eps for q in sq]
    sq_big = [2.5 * q for q in sq]
    product = [a * b for a, b in zip(second[:-1], second[1:])]
    prod_outer = [2.75 * q for q in product]
    prod_inner = [1.25 * q for q in product]
    rights, lefts = [], []
    for k in range(n + 1):
        s1 = (sq_big[k + 1] - prod_outer[k]) + sq_eps[k]
        s2 = (sq[k + 1] - prod_inner[k + 1]) + sq_eps[k + 2]
        s3 = (sq_big[k + 2] - prod_outer[k + 2]) + sq_eps[k + 3]
        right, left = corrections(s1, s2, s3, fourth[k], fourth[k + 1])
        rights.append(right)
        lefts.append(left)
    sums, gaps = [], []
    for i in range(n):
        right, left = rights[i], lefts[i + 1]
        central = 6.0 * (diff[i + 2] + diff[i + 3]) - (second[i + 3] - second[i + 1])
        sums.append(central + (left - right))
        gaps.append((left + right) - fourth[i + 1])
    return sums, gaps


def edge_correction(g, eps):
    s = g * g + eps
    return (3.0 * eps * eps) * g / (7.0 * (s * s) + 3.0 * eps * eps)


def turn_slopes(cells, eps):
    d0, d1, d2 = (b - a for a, b in zip(cells[:-1], cells[1:]))
    e1 = d1 - d0
    e2 = d2 - d1
    sq1, sq2, p12 = e1 * e1, e2 * e2, e1 * e2
    big1, big2 = 2.5 * sq1, 2.5 * sq2
    one1, one2 = sq1 + eps, sq2 + eps
    x0, x1, x2, x3 = e1, e2 - (e1 + e1), e1 - (e2 + e2), e2
    outer = 2.75 * p12
    right_edge = edge_correction(e1, eps)
    left_edge = edge_correction(e2, eps)
    r0, l0 = corrections(eps, one1, (big1 - outer) + one2, x0, x1)
    r1, l1 = corrections(big1 + eps, (sq1 - 1.25 * p12) + one2, big2 + eps, x1, x2)
    r2, l2 = corrections((big2 - outer) + one1, one2, eps, x2, x3)
    rights, lefts = (right_edge, r0, r1, r2), (l0, l1, l2, left_edge)
    centrals = (
        12.0 * d0 - e1,
        6.0 * (d0 + d1) - e2,
        6.0 * (d1 + d2) + e1,
        12.0 * d2 + e2,
    )
    sums = [c + (le - ri) for c, le, ri in zip(centrals, lefts, rights)]
    gaps = [(le + ri) - x for x, le, ri in zip((x0, x1, x2, x3), lefts, rights)]
    return sums, gaps


def lane_corrections(em, e, ep, epp, eps):
    tm, t, tp = e - em, ep - e, epp - ep
    sq, sqp = e * e, ep * ep
    sqp_eps = sqp + eps
    s1 = e * (2.5 * e - 2.75 * em) + (em * em + eps)
    s2 = e * (e - 1.25 * ep) + sqp_eps
    s3 = ep * (2.5 * ep - 2.75 * epp) + (epp * epp + eps)
    x1 = t - tm
    right, left = corrections(s1, s2, s3, x1, tp - t)
    return right, left, x1


def heading_slopes(f, lane):
    place = lane % HEADINGS

    def moved(v, by):
        near = pltpu.roll(v, (-by) % LANE, 1)
        wrapped = pltpu.roll(v, (HEADINGS - by if by > 0 else -HEADINGS - by) % LANE, 1)
        inside = place < HEADINGS - by if by > 0 else place >= -by
        return jnp.where(inside, near, wrapped)

    d = moved(f, 1) - f
    dm = moved(d, -1)
    e = d - dm
    em, ep, epp = moved(e, -1), moved(e, 1), moved(e, 2)
    right, left, x1 = lane_corrections(em, e, ep, epp, EPS_HEADING)
    right = moved(right, -1)
    return 6.0 * (d + dm) - (ep - em) + (left - right), (left + right) - x1


def speed_slopes(pair, lane):
    first = lane < HEADINGS
    last = lane >= LANE - HEADINGS

    def up(vs):
        r0, r1 = (pltpu.roll(v, LANE - HEADINGS, 1) for v in vs)
        return jnp.where(last, r1, r0), jnp.where(last, r0, r1)

    def down(vs):
        r0, r1 = (pltpu.roll(v, HEADINGS, 1) for v in vs)
        return jnp.where(first, r1, r0), jnp.where(first, r0, r1)

    d = [b - a for a, b in zip(pair, up(pair))]
    dm = list(down(d))
    d[1] = jnp.where(last, dm[1], d[1])
    dm[0] = jnp.where(first, d[0], dm[0])
    e = [a - b for a, b in zip(d, dm)]
    em = down(e)
    ep = up(e)
    epp = list(up(ep))
    epp[1] = jnp.where(last, 0.0, epp[1])
    out = [lane_corrections(em[k], e[k], ep[k], epp[k], EPS_XY) for k in range(2)]
    rights = list(down((out[0][0], out[1][0])))
    rights[0] = jnp.where(first, edge_correction(ep[0], EPS_XY), rights[0])
    sums = [
        6.0 * (d[k] + dm[k]) - (ep[k] - em[k]) + (out[k][1] - rights[k]) for k in range(2)
    ]
    gaps = [(out[k][1] + rights[k]) - out[k][2] for k in range(2)]
    return sums, gaps


def kernel(
    gx_count,
    gy_count,
    u_ref,
    dist_ref,
    coord_ref,
    out_ref,
    frame,
    flat,
    px,
    qx,
    qy,
    ham,
    alpha,
    peak,
    arsend,
    arrecv,
    send_sem,
    recv_sem,
    ar_send_sem,
    ar_recv_sem,
):
    gx = lax.axis_index("gx")
    gy = lax.axis_index("gy")

    barrier = pltpu.get_barrier_semaphore()
    for count, axis in ((gx_count, 0), (gy_count, 1)):

        @pl.loop(1, count)
        def _(k, count=count, axis=axis):
            where = (lax.rem(gx + k, count), gy) if axis == 0 else (gx, lax.rem(gy + k, count))
            pl.semaphore_signal(barrier, inc=1, device_id=where, device_id_type=MESH)

    lane = lax.broadcasted_iota(jnp.int32, (SUB, LANE), 1)

    def cell(s, x, y):
        return (s * FX + x, pl.ds(y * SUB, SUB), slice(None))

    for x in range(NX):
        for j in range(TILES):
            tile = u_ref[x, :, j * LANE : (j + 1) * LANE]
            frame[3 + x, pl.ds(3 * SUB + j, SUB, stride=SUB), :] = SCALE * tile

    def flat_pass(s):
        @pl.loop(0, NX)
        def _(x):
            row = s * FX + 3 + x
            tiles = [frame[row, pl.ds(3 * SUB + j, SUB, stride=SUB), :] for j in range(TILES)]
            parts = [None] * TILES
            for j in range(TILES):
                total, gap = heading_slopes(tiles[j], lane)
                rate = 0.1 * (j // 2 - (TURNS - 1) / 2.0)
                parts[j] = (turn_peak / (12.0 * step_heading)) * gap - (
                    rate / (12.0 * step_heading)
                ) * total
            for c in range(TURNS):
                sums, gaps = speed_slopes(tiles[2 * c : 2 * c + 2], lane)
                for k in range(2):
                    parts[2 * c + k] += (accel / (12.0 * step_xy)) * (gaps[k] - jnp.abs(sums[k]))
            for k in range(2):
                sums, gaps = turn_slopes(tiles[k::2], EPS_XY)
                for c in range(TURNS):
                    parts[2 * c + k] += (torque / (12.0 * step_xy)) * (gaps[c] - jnp.abs(sums[c]))
            for j in range(TILES):
                flat[x, pl.ds(j, SUB, stride=SUB), :] = parts[j]

    def halo(s, way):
        row = s * FX
        if way < 2:
            src = frame.at[pl.ds(row + (4 if way == 0 else 3), 3), pl.ds(3 * SUB, NY * SUB)]
            dst = frame.at[pl.ds(row + (0 if way == 0 else 3 + NX), 3), pl.ds(3 * SUB, NY * SUB)]
            where = (gx + 1, gy) if way == 0 else (gx - 1, gy)
        else:
            src = frame.at[pl.ds(row + 3, NX), pl.ds((NY if way == 2 else 3) * SUB, 3 * SUB)]
            dst = frame.at[
                pl.ds(row + 3, NX), pl.ds((0 if way == 2 else 3 + NY) * SUB, 3 * SUB)
            ]
            where = (gx, gy + 1) if way == 2 else (gx, gy - 1)
        return pltpu.make_async_remote_copy(
            src_ref=src,
            dst_ref=dst,
            send_sem=send_sem.at[s, way],
            recv_sem=recv_sem.at[s, way],
            device_id=where,
            device_id_type=MESH,
        )

    sends = (gx < gx_count - 1, gx > 0, gy < gy_count - 1, gy > 0)
    receives = (gx > 0, gx < gx_count - 1, gy > 0, gy < gy_count - 1)

    def send_halos(s):
        for way in range(4):

            @pl.when(sends[way])
            def _(way=way):
                halo(s, way).start()

    def wait_halos(s):
        for way in range(4):

            @pl.when(receives[way])
            def _(way=way):
                halo(s, way).wait_recv()

            @pl.when(sends[way])
            def _(way=way):
                halo(s, way).wait_send()

    def fill_ghosts(s):
        for low, outside in ((True, gx == 0), (False, gx == gx_count - 1)):

            @pl.when(outside)
            def _(low=low):
                end, inner, step = (3, 4, -1) if low else (2 + NX, 1 + NX, 1)

                @pl.loop(0, NY)
                def _(y):
                    edge = frame[cell(s, end, 3 + y)]
                    slope = edge - frame[cell(s, inner, 3 + y)]
                    for k in (1, 2, 3):
                        frame[cell(s, end + step * k, 3 + y)] = edge + float(k) * slope

        for low, outside in ((True, gy == 0), (False, gy == gy_count - 1)):

            @pl.when(outside)
            def _(low=low):
                end, inner, step = (3, 4, -1) if low else (2 + NY, 1 + NY, 1)

                @pl.loop(0, NX)
                def _(x):
                    edge = frame[cell(s, 3 + x, end)]
                    slope = edge - frame[cell(s, 3 + x, inner)]
                    for k in (1, 2, 3):
                        frame[cell(s, 3 + x, end + step * k)] = edge + float(k) * slope

    def position_pass(s):
        @pl.loop(0, NY)
        def _(y):
            sums, gaps = line_slopes([frame[cell(s, i, 3 + y)] for i in range(FX)], EPS_XY)
            for x in range(NX):
                px[x, pl.ds(y * SUB, SUB), :] = sums[x]
                qx[x, pl.ds(y * SUB, SUB), :] = gaps[x]

        @pl.loop(0, NX)
        def _(x):
            sums, gaps = line_slopes([frame[cell(s, 3 + x, i)] for i in range(FY)], EPS_XY)
            vx = coord_ref[0]
            vy = coord_ref[1]
            top_x, top_y = peak[0], peak[1]
            for y in range(NY):
                at = (x, pl.ds(y * SUB, SUB), slice(None))
                bound = dist_ref[x, y]
                sx, sy = px[at], sums[y]
                square = sx * sx + sy * sy + RADIUS
                inverse = lax.rsqrt(square)
                pull = bound * inverse
                top_x = jnp.maximum(top_x, jnp.abs(vx - pull * sx))
                top_y = jnp.maximum(top_y, jnp.abs(vy - pull * sy))
                ham[at] = flat[at] + (1.0 / (12.0 * step_xy)) * (
                    (pull * square) - (sx * vx + sy * vy)
                )
                qy[at] = gaps[y]
            peak[0] = top_x
            peak[1] = top_y

    half = lane < LANE // 2

    def fold(v):
        for by in (4, 2, 1):
            v = jnp.maximum(v, pltpu.roll(v, by, 0))
        return jnp.maximum(v, pltpu.roll(v, LANE // 2, 1))

    def ar_copy(turn, phase, k):
        count = gy_count if phase == 0 else gx_count
        where = (gx, lax.rem(gy + k, count)) if phase == 0 else (lax.rem(gx + k, count), gy)
        return pltpu.make_async_remote_copy(
            src_ref=arsend.at[2 * turn + phase],
            dst_ref=arrecv.at[2 * turn + phase, k - 1],
            send_sem=ar_send_sem.at[2 * turn + phase],
            recv_sem=ar_recv_sem.at[2 * turn + phase],
            device_id=where,
            device_id_type=MESH,
        )

    def ar_start(turn, phase, row):
        arsend[2 * turn + phase] = row

        @pl.loop(1, gy_count if phase == 0 else gx_count)
        def _(k):
            ar_copy(turn, phase, k).start()

    def ar_finish(turn, phase):
        count = gy_count if phase == 0 else gx_count
        slot = 2 * turn + phase
        every = arrecv.at[slot, pl.ds(0, count - 1)]
        whole = pltpu.make_async_remote_copy(
            src_ref=every,
            dst_ref=every,
            send_sem=ar_send_sem.at[slot],
            recv_sem=ar_recv_sem.at[slot],
            device_id=(gx, gy),
            device_id_type=MESH,
        )
        whole.wait_send()
        whole.wait_recv()
        row = arsend[slot]
        for k in range(count - 1):
            row = jnp.maximum(row, arrecv[slot, k])
        return row

    def own_row():
        return jnp.where(half, fold(peak[0]), fold(peak[1]))[0:1]

    def set_alpha(row):
        row = jnp.broadcast_to(row, (SUB, LANE))
        ax = jnp.max(jnp.where(half, row, 0.0), axis=1, keepdims=True)
        ay = jnp.max(jnp.where(half, 0.0, row), axis=1, keepdims=True)
        ax = jnp.broadcast_to(ax, (SUB, LANE))
        ay = jnp.broadcast_to(ay, (SUB, LANE))
        total = ax / step_xy + ay / step_xy + turn_peak / step_heading
        alpha[0] = (1.0 / (12.0 * step_xy)) * ax
        alpha[1] = (1.0 / (12.0 * step_xy)) * ay
        alpha[2] = 0.75 / (total + accel / step_xy + torque / step_xy)

    peak[...] = jnp.zeros_like(peak)

    @pl.loop(0, 6)
    def _(s):
        part = lax.rem(s, 3)
        flat_pass(s)
        fill_ghosts(s)

        @pl.when(s == 0)
        def _():
            pl.semaphore_wait(barrier, gx_count + gy_count - 2)
            send_halos(s)

        @pl.when(s == 3)
        def _():
            ar_start(1, 1, ar_finish(1, 0))

        wait_halos(s)
        position_pass(s)

        @pl.when(s == 0)
        def _():
            ar_start(0, 0, own_row())
            ar_start(0, 1, ar_finish(0, 0))
            set_alpha(ar_finish(0, 1))
            peak[...] = jnp.zeros_like(peak)

        @pl.when(s == 2)
        def _():
            ar_start(1, 0, own_row())

        @pl.when(s == 3)
        def _():
            set_alpha(ar_finish(1, 1))

        keep = jnp.where(part == 0, 0.0, jnp.where(part == 1, 0.75, 1.0 / 3.0))
        take = jnp.where(part == 0, 1.0, jnp.where(part == 1, 0.25, 2.0 / 3.0))
        base = s - part

        @pl.loop(0, NX)
        def _(x):
            ax, ay, dt = alpha[0], alpha[1], alpha[2]
            for y in range(NY):
                at = (x, pl.ds(y * SUB, SUB), slice(None))
                rate = ham[at] + (ax * qx[at] + ay * qy[at])
                moved = frame[cell(s, 3 + x, 3 + y)] + dt * rate
                frame[cell(s + 1, 3 + x, 3 + y)] = (
                    keep * frame[cell(base, 3 + x, 3 + y)] + take * moved
                )

        @pl.when(s < 5)
        def _():
            send_halos(s + 1)

    for x in range(NX):
        for j in range(TILES):
            tile = frame[6 * FX + 3 + x, pl.ds(3 * SUB + j, SUB, stride=SUB), :]
            out_ref[x, :, j * LANE : (j + 1) * LANE] = (1.0 / SCALE) * tile


def body(gx_count, gy_count, initial_value, disturbance):
    most = max(gx_count, gy_count)
    return pl.pallas_call(
        functools.partial(kernel, gx_count, gy_count),
        out_shape=jax.ShapeDtypeStruct((NX, NY, LANES), jnp.float32),
        in_specs=[
            pl.BlockSpec(memory_space=pltpu.VMEM),
            pl.BlockSpec(memory_space=pltpu.SMEM),
            pl.BlockSpec(memory_space=pltpu.VMEM),
        ],
        out_specs=pl.BlockSpec(memory_space=pltpu.VMEM),
        scratch_shapes=[
            pltpu.VMEM((7 * FX, FY * SUB, LANE), jnp.float32),
            pltpu.VMEM((NX, NY * SUB, LANE), jnp.float32),
            pltpu.VMEM((NX, NY * SUB, LANE), jnp.float32),
            pltpu.VMEM((NX, NY * SUB, LANE), jnp.float32),
            pltpu.VMEM((NX, NY * SUB, LANE), jnp.float32),
            pltpu.VMEM((NX, NY * SUB, LANE), jnp.float32),
            pltpu.VMEM((3, SUB, LANE), jnp.float32),
            pltpu.VMEM((2, SUB, LANE), jnp.float32),
            pltpu.VMEM((4, 1, LANE), jnp.float32),
            pltpu.VMEM((4, most - 1, 1, LANE), jnp.float32),
            pltpu.SemaphoreType.DMA((6, 4)),
            pltpu.SemaphoreType.DMA((6, 4)),
            pltpu.SemaphoreType.DMA((4,)),
            pltpu.SemaphoreType.DMA((4,)),
        ],
        compiler_params=pltpu.CompilerParams(collective_id=0, has_side_effects=True),
    )(initial_value, disturbance, jnp.asarray(coordinate_tables()))


def solution(mesh):
    placed = (P("gx", "gy", None), P("gx", "gy"))
    return jax.shard_map(
        functools.partial(body, mesh.shape["gx"], mesh.shape["gy"]),
        mesh=mesh,
        in_specs=placed,
        out_specs=P("gx", "gy", None),
        check_vma=False,
    )
```

```python
import functools
import math

import jax
import jax.numpy as jnp
import numpy as np
from jax import lax
from jax.experimental import pallas as pl
from jax.experimental.pallas import tpu as pltpu
from jax.sharding import PartitionSpec as P

HEADINGS = 16
SPEEDS = 16
TURNS = 4
LANES = HEADINGS * SPEEDS * TURNS

NX = 4
NY = 8
SUB = 8
LANE = 128
TILES = LANES // LANE
FX = NX + 6
FY = NY + 6

SCALE = 4.0
step_xy = 0.1
step_heading = 2.0 * math.pi / HEADINGS
accel = 0.5
torque = 0.3
turn_peak = 0.1 * (TURNS - 1) / 2.0
EPS_XY = 0.75e-6 * (SCALE * step_xy) ** 2
EPS_HEADING = 0.75e-6 * (SCALE * step_heading) ** 2
RADIUS = 0.01 * (SCALE * 12.0 * step_xy) ** 2

MESH = pl.DeviceIdType.MESH


def coordinate_tables():
    lanes = np.arange(LANES)
    heading = (-math.pi + ((lanes % HEADINGS) + 0.5) * step_heading).astype(np.float32)
    speed = (1.0 + 0.1 * (lanes // HEADINGS % SPEEDS)).astype(np.float32)
    vx = speed * np.cos(heading)
    vy = speed * np.sin(heading)
    return np.stack([vx, vy]).astype(np.float32).reshape(2, SUB, LANE)


def corrections(s1, s2, s3, x1, x2):
    a = s2 * s3
    b = s1 * s3
    c = s1 * s2
    r1 = a * a
    r2 = b * b
    r3 = c * c
    mid = r1 + r3 + 6.0 * r2
    den_right = mid + (r3 + r3)
    den_left = mid + (r1 + r1)
    y1 = r1 * x1
    y2 = r3 * x2
    both = y1 + y2
    both = both + both
    right = (both + y2) / den_right
    left = (both + y1) / den_left
    return right, left


def smooth_outer(inner, outer_sq, inner_sq, product):
    return (2.5 * inner_sq - 2.75 * product) + outer_sq


def line_slopes(cells, eps):
    n = len(cells) - 6
    diff = [b - a for a, b in zip(cells[:-1], cells[1:])]
    second = [b - a for a, b in zip(diff[:-1], diff[1:])]
    third = [b - a for a, b in zip(second[:-1], second[1:])]
    fourth = [b - a for a, b in zip(third[:-1], third[1:])]
    sq = [e * e for e in second]
    sq_eps = [q + eps for q in sq]
    sq_big = [2.5 * q for q in sq]
    product = [a * b for a, b in zip(second[:-1], second[1:])]
    prod_outer = [2.75 * q for q in product]
    prod_inner = [1.25 * q for q in product]
    rights, lefts = [], []
    for k in range(n + 1):
        s1 = (sq_big[k + 1] - prod_outer[k]) + sq_eps[k]
        s2 = (sq[k + 1] - prod_inner[k + 1]) + sq_eps[k + 2]
        s3 = (sq_big[k + 2] - prod_outer[k + 2]) + sq_eps[k + 3]
        right, left = corrections(s1, s2, s3, fourth[k], fourth[k + 1])
        rights.append(right)
        lefts.append(left)
    sums, gaps = [], []
    for i in range(n):
        right, left = rights[i], lefts[i + 1]
        central = 6.0 * (diff[i + 2] + diff[i + 3]) - (second[i + 3] - second[i + 1])
        sums.append(central + (left - right))
        gaps.append((left + right) - fourth[i + 1])
    return sums, gaps


def edge_correction(g, eps):
    s = g * g + eps
    return (3.0 * eps * eps) * g / (7.0 * (s * s) + 3.0 * eps * eps)


def turn_slopes(cells, eps):
    d0, d1, d2 = (b - a for a, b in zip(cells[:-1], cells[1:]))
    e1 = d1 - d0
    e2 = d2 - d1
    sq1, sq2, p12 = e1 * e1, e2 * e2, e1 * e2
    big1, big2 = 2.5 * sq1, 2.5 * sq2
    one1, one2 = sq1 + eps, sq2 + eps
    x0, x1, x2, x3 = e1, e2 - (e1 + e1), e1 - (e2 + e2), e2
    outer = 2.75 * p12
    right_edge = edge_correction(e1, eps)
    left_edge = edge_correction(e2, eps)
    r0, l0 = corrections(eps, one1, (big1 - outer) + one2, x0, x1)
    r1, l1 = corrections(big1 + eps, (sq1 - 1.25 * p12) + one2, big2 + eps, x1, x2)
    r2, l2 = corrections((big2 - outer) + one1, one2, eps, x2, x3)
    rights, lefts = (right_edge, r0, r1, r2), (l0, l1, l2, left_edge)
    centrals = (
        12.0 * d0 - e1,
        6.0 * (d0 + d1) - e2,
        6.0 * (d1 + d2) + e1,
        12.0 * d2 + e2,
    )
    sums = [c + (le - ri) for c, le, ri in zip(centrals, lefts, rights)]
    gaps = [(le + ri) - x for x, le, ri in zip((x0, x1, x2, x3), lefts, rights)]
    return sums, gaps


def lane_corrections(em, e, ep, epp, eps):
    tm, t, tp = e - em, ep - e, epp - ep
    sq, sqp = e * e, ep * ep
    sqp_eps = sqp + eps
    s1 = e * (2.5 * e - 2.75 * em) + (em * em + eps)
    s2 = e * (e - 1.25 * ep) + sqp_eps
    s3 = ep * (2.5 * ep - 2.75 * epp) + (epp * epp + eps)
    x1 = t - tm
    right, left = corrections(s1, s2, s3, x1, tp - t)
    return right, left, x1


def heading_slopes(f, lane):
    place = lane % HEADINGS

    def moved(v, by):
        near = pltpu.roll(v, (-by) % LANE, 1)
        wrapped = pltpu.roll(v, (HEADINGS - by if by > 0 else -HEADINGS - by) % LANE, 1)
        inside = place < HEADINGS - by if by > 0 else place >= -by
        return jnp.where(inside, near, wrapped)

    d = moved(f, 1) - f
    dm = moved(d, -1)
    e = d - dm
    em, ep, epp = moved(e, -1), moved(e, 1), moved(e, 2)
    right, left, x1 = lane_corrections(em, e, ep, epp, EPS_HEADING)
    right = moved(right, -1)
    return 6.0 * (d + dm) - (ep - em) + (left - right), (left + right) - x1


def speed_slopes(pair, lane):
    first = lane < HEADINGS
    last = lane >= LANE - HEADINGS

    def up(vs):
        r0, r1 = (pltpu.roll(v, LANE - HEADINGS, 1) for v in vs)
        return jnp.where(last, r1, r0), jnp.where(last, r0, r1)

    def down(vs):
        r0, r1 = (pltpu.roll(v, HEADINGS, 1) for v in vs)
        return jnp.where(first, r1, r0), jnp.where(first, r0, r1)

    d = [b - a for a, b in zip(pair, up(pair))]
    dm = list(down(d))
    d[1] = jnp.where(last, dm[1], d[1])
    dm[0] = jnp.where(first, d[0], dm[0])
    e = [a - b for a, b in zip(d, dm)]
    em = down(e)
    ep = up(e)
    epp = list(up(ep))
    epp[1] = jnp.where(last, 0.0, epp[1])
    out = [lane_corrections(em[k], e[k], ep[k], epp[k], EPS_XY) for k in range(2)]
    rights = list(down((out[0][0], out[1][0])))
    rights[0] = jnp.where(first, edge_correction(ep[0], EPS_XY), rights[0])
    sums = [
        6.0 * (d[k] + dm[k]) - (ep[k] - em[k]) + (out[k][1] - rights[k]) for k in range(2)
    ]
    gaps = [(out[k][1] + rights[k]) - out[k][2] for k in range(2)]
    return sums, gaps


def kernel(
    gx_count,
    gy_count,
    u_hbm,
    dist_hbm,
    coord_hbm,
    out_ref,
    u_ref,
    dist_ref,
    coord_ref,
    frame,
    flat,
    py,
    qx,
    qy,
    ham,
    alpha,
    peak,
    arsend,
    arrecv,
    load_sem,
    send_x_sem,
    recv_x_sem,
    send_y_sem,
    recv_y_sem,
    ar_send_sem,
    ar_recv_sem,
):
    gx = lax.axis_index("gx")
    gy = lax.axis_index("gy")

    loads = [
        pltpu.make_async_copy(src, dst, load_sem.at[k])
        for k, (src, dst) in enumerate(
            ((u_hbm, u_ref), (dist_hbm, dist_ref), (coord_hbm, coord_ref))
        )
    ]
    for load in loads:
        load.start()

    barrier = pltpu.get_barrier_semaphore()
    for count, axis in ((gx_count, 0), (gy_count, 1)):

        @pl.loop(1, count)
        def _(k, count=count, axis=axis):
            where = (lax.rem(gx + k, count), gy) if axis == 0 else (gx, lax.rem(gy + k, count))
            pl.semaphore_signal(barrier, inc=1, device_id=where, device_id_type=MESH)

    lane = lax.broadcasted_iota(jnp.int32, (SUB, LANE), 1)

    def cell(s, x, y):
        return (s * FX + x, pl.ds(y * SUB, SUB), slice(None))

    for load in loads:
        load.wait()

    for x in range(NX):
        for j in range(TILES):
            tile = u_ref[x, :, j * LANE : (j + 1) * LANE]
            frame[3 + x, pl.ds(3 * SUB + j, SUB, stride=SUB), :] = SCALE * tile

    def flat_pass(s):
        @pl.loop(0, NX)
        def _(x):
            row = s * FX + 3 + x
            tiles = [frame[row, pl.ds(3 * SUB + j, SUB, stride=SUB), :] for j in range(TILES)]
            parts = [None] * TILES
            for j in range(TILES):
                total, gap = heading_slopes(tiles[j], lane)
                rate = 0.1 * (j // 2 - (TURNS - 1) / 2.0)
                parts[j] = (turn_peak / (12.0 * step_heading)) * gap - (
                    rate / (12.0 * step_heading)
                ) * total
            for c in range(TURNS):
                sums, gaps = speed_slopes(tiles[2 * c : 2 * c + 2], lane)
                for k in range(2):
                    parts[2 * c + k] += (accel / (12.0 * step_xy)) * (gaps[k] - jnp.abs(sums[k]))
            for k in range(2):
                sums, gaps = turn_slopes(tiles[k::2], EPS_XY)
                for c in range(TURNS):
                    parts[2 * c + k] += (torque / (12.0 * step_xy)) * (gaps[c] - jnp.abs(sums[c]))
            for j in range(TILES):
                flat[x, pl.ds(j, SUB, stride=SUB), :] = parts[j]

    sends = (gx < gx_count - 1, gx > 0, gy < gy_count - 1, gy > 0)
    receives = (gx > 0, gx < gx_count - 1, gy > 0, gy < gy_count - 1)

    def halo_x(s, way, y):
        row = s * FX
        turn = lax.rem(s, 2)
        at = pl.ds((3 + y) * SUB, SUB)
        return pltpu.make_async_remote_copy(
            src_ref=frame.at[pl.ds(row + (4 if way == 0 else 3), 3), at],
            dst_ref=frame.at[pl.ds(row + (0 if way == 0 else 3 + NX), 3), at],
            send_sem=send_x_sem.at[turn, way, y],
            recv_sem=recv_x_sem.at[turn, way, y],
            device_id=(gx + 1, gy) if way == 0 else (gx - 1, gy),
            device_id_type=MESH,
        )

    def halo_y(s, way):
        rows = pl.ds(s * FX + 3, NX)
        turn = lax.rem(s, 2)
        return pltpu.make_async_remote_copy(
            src_ref=frame.at[rows, pl.ds((NY if way == 0 else 3) * SUB, 3 * SUB)],
            dst_ref=frame.at[rows, pl.ds((0 if way == 0 else 3 + NY) * SUB, 3 * SUB)],
            send_sem=send_y_sem.at[turn, way],
            recv_sem=recv_y_sem.at[turn, way],
            device_id=(gx, gy + 1) if way == 0 else (gx, gy - 1),
            device_id_type=MESH,
        )

    def column(i):
        return jnp.where(i < 3, i, jnp.where(i < 6, i + 2, i - 3))

    def send_column(s, y):
        for way in range(2):

            @pl.when(sends[way])
            def _(way=way):
                halo_x(s, way, y).start()

    def send_rows(s, i):
        @pl.when(jnp.logical_and(i == 2, sends[3]))
        def _():
            halo_y(s, 1).start()

        @pl.when(jnp.logical_and(i == 5, sends[2]))
        def _():
            halo_y(s, 0).start()

    def finish_sends(s):
        for way in range(2):

            @pl.when(sends[way])
            def _(way=way):
                @pl.loop(0, NY)
                def _(y):
                    halo_x(s, way, y).wait_send()

            @pl.when(sends[2 + way])
            def _(way=way):
                halo_y(s, way).wait_send()

    def fill_ghosts(s):
        for low, outside in ((True, gx == 0), (False, gx == gx_count - 1)):

            @pl.when(outside)
            def _(low=low):
                end, inner, step = (3, 4, -1) if low else (2 + NX, 1 + NX, 1)

                @pl.loop(0, NY)
                def _(y):
                    edge = frame[cell(s, end, 3 + y)]
                    slope = edge - frame[cell(s, inner, 3 + y)]
                    for k in (1, 2, 3):
                        frame[cell(s, end + step * k, 3 + y)] = edge + float(k) * slope

        for low, outside in ((True, gy == 0), (False, gy == gy_count - 1)):

            @pl.when(outside)
            def _(low=low):
                end, inner, step = (3, 4, -1) if low else (2 + NY, 1 + NY, 1)

                @pl.loop(0, NX)
                def _(x):
                    edge = frame[cell(s, 3 + x, end)]
                    slope = edge - frame[cell(s, 3 + x, inner)]
                    for k in (1, 2, 3):
                        frame[cell(s, 3 + x, end + step * k)] = edge + float(k) * slope

    def second_pass(s):
        for way in range(2):

            @pl.when(receives[2 + way])
            def _(way=way):
                halo_y(s, way).wait_recv()

        @pl.loop(0, NX)
        def _(x):
            sums, gaps = line_slopes([frame[cell(s, 3 + x, i)] for i in range(FY)], EPS_XY)
            for y in range(NY):
                py[x, pl.ds(y * SUB, SUB), :] = sums[y]
                qy[x, pl.ds(y * SUB, SUB), :] = gaps[y]

    def first_slopes(s, y):
        for way in range(2):

            @pl.when(receives[way])
            def _(way=way):
                halo_x(s, way, y).wait_recv()

        sums, gaps = line_slopes([frame[cell(s, i, 3 + y)] for i in range(FX)], EPS_XY)
        vx = coord_ref[0]
        vy = coord_ref[1]
        top_x, top_y = peak[0], peak[1]
        rates = []
        for x in range(NX):
            at = (x, pl.ds(y * SUB, SUB), slice(None))
            bound = dist_ref[x, y]
            sx, sy = sums[x], py[at]
            square = sx * sx + sy * sy + RADIUS
            pull = bound * lax.rsqrt(square)
            top_x = jnp.maximum(top_x, jnp.abs(vx - pull * sx))
            top_y = jnp.maximum(top_y, jnp.abs(vy - pull * sy))
            rates.append(
                flat[at] + (1.0 / (12.0 * step_xy)) * ((pull * square) - (sx * vx + sy * vy))
            )
        peak[0] = top_x
        peak[1] = top_y
        return rates, gaps

    half = lane < LANE // 2

    def fold(v):
        for by in (4, 2, 1):
            v = jnp.maximum(v, pltpu.roll(v, by, 0))
        return jnp.maximum(v, pltpu.roll(v, LANE // 2, 1))

    def ar_copy(turn, phase, k):
        count = gy_count if phase == 0 else gx_count
        where = (gx, lax.rem(gy + k, count)) if phase == 0 else (lax.rem(gx + k, count), gy)
        return pltpu.make_async_remote_copy(
            src_ref=arsend.at[2 * turn + phase],
            dst_ref=arrecv.at[2 * turn + phase, k - 1],
            send_sem=ar_send_sem.at[2 * turn + phase],
            recv_sem=ar_recv_sem.at[2 * turn + phase],
            device_id=where,
            device_id_type=MESH,
        )

    def ar_start(turn, phase, row):
        arsend[2 * turn + phase] = row

        @pl.loop(1, gy_count if phase == 0 else gx_count)
        def _(k):
            ar_copy(turn, phase, k).start()

    def ar_finish(turn, phase):
        count = gy_count if phase == 0 else gx_count
        slot = 2 * turn + phase
        every = arrecv.at[slot, pl.ds(0, count - 1)]
        whole = pltpu.make_async_remote_copy(
            src_ref=every,
            dst_ref=every,
            send_sem=ar_send_sem.at[slot],
            recv_sem=ar_recv_sem.at[slot],
            device_id=(gx, gy),
            device_id_type=MESH,
        )
        whole.wait_send()
        whole.wait_recv()
        row = arsend[slot]
        for k in range(count - 1):
            row = jnp.maximum(row, arrecv[slot, k])
        return row

    def own_row():
        return jnp.where(half, fold(peak[0]), fold(peak[1]))[0:1]

    def set_alpha(row):
        row = jnp.broadcast_to(row, (SUB, LANE))
        ax = jnp.max(jnp.where(half, row, 0.0), axis=1, keepdims=True)
        ay = jnp.max(jnp.where(half, 0.0, row), axis=1, keepdims=True)
        ax = jnp.broadcast_to(ax, (SUB, LANE))
        ay = jnp.broadcast_to(ay, (SUB, LANE))
        total = ax / step_xy + ay / step_xy + turn_peak / step_heading
        alpha[0] = (1.0 / (12.0 * step_xy)) * ax
        alpha[1] = (1.0 / (12.0 * step_xy)) * ay
        alpha[2] = 0.75 / (total + accel / step_xy + torque / step_xy)

    peak[...] = jnp.zeros_like(peak)

    @pl.loop(0, 6)
    def _(s):
        part = lax.rem(s, 3)
        base = s - part
        keep = jnp.where(part == 0, 0.0, jnp.where(part == 1, 0.75, 1.0 / 3.0))
        take = jnp.where(part == 0, 1.0, jnp.where(part == 1, 0.25, 2.0 / 3.0))

        flat_pass(s)
        fill_ghosts(s)

        @pl.when(s == 0)
        def _():
            pl.semaphore_wait(barrier, gx_count + gy_count - 2)

            @pl.loop(0, NY)
            def _(i):
                send_column(s, column(i))
                send_rows(s, i)

        second_pass(s)

        @pl.when(s == 3)
        def _():
            ar_start(1, 1, ar_finish(1, 0))

        def advance(y, rates, gaps):
            ax, ay, dt = alpha[0], alpha[1], alpha[2]
            for x in range(NX):
                at = (x, pl.ds(y * SUB, SUB), slice(None))
                rate = rates[x] + (ax * gaps[x] + ay * qy[at])
                moved = frame[cell(s, 3 + x, 3 + y)] + dt * rate
                frame[cell(s + 1, 3 + x, 3 + y)] = (
                    keep * frame[cell(base, 3 + x, 3 + y)] + take * moved
                )

        def send_next(i, y):
            @pl.when(s < 5)
            def _():
                send_column(s + 1, y)
                send_rows(s + 1, i)

        @pl.when(part > 0)
        def _():
            @pl.loop(0, NY)
            def _(i):
                y = column(i)
                advance(y, *first_slopes(s, y))
                send_next(i, y)

        @pl.when(part == 0)
        def _():
            @pl.loop(0, NY)
            def _(y):
                rates, gaps = first_slopes(s, y)
                for x in range(NX):
                    at = (x, pl.ds(y * SUB, SUB), slice(None))
                    ham[at] = rates[x]
                    qx[at] = gaps[x]

            @pl.when(s == 0)
            def _():
                ar_start(0, 0, own_row())
                ar_start(0, 1, ar_finish(0, 0))
                set_alpha(ar_finish(0, 1))
                peak[...] = jnp.zeros_like(peak)

            @pl.when(s == 3)
            def _():
                set_alpha(ar_finish(1, 1))

            @pl.loop(0, NY)
            def _(i):
                y = column(i)
                at = [(x, pl.ds(y * SUB, SUB), slice(None)) for x in range(NX)]
                advance(y, [ham[a] for a in at], [qx[a] for a in at])
                send_next(i, y)

        @pl.when(s == 2)
        def _():
            ar_start(1, 0, own_row())

        finish_sends(s)

    for x in range(NX):
        for j in range(TILES):
            tile = frame[6 * FX + 3 + x, pl.ds(3 * SUB + j, SUB, stride=SUB), :]
            out_ref[x, :, j * LANE : (j + 1) * LANE] = (1.0 / SCALE) * tile


def body(gx_count, gy_count, initial_value, disturbance):
    most = max(gx_count, gy_count)
    return pl.pallas_call(
        functools.partial(kernel, gx_count, gy_count),
        out_shape=jax.ShapeDtypeStruct((NX, NY, LANES), jnp.float32),
        in_specs=[pl.BlockSpec(memory_space=pl.ANY)] * 3,
        out_specs=pl.BlockSpec(memory_space=pltpu.VMEM),
        scratch_shapes=[
            pltpu.VMEM((NX, NY, LANES), jnp.float32),
            pltpu.SMEM((NX, NY), jnp.float32),
            pltpu.VMEM((2, SUB, LANE), jnp.float32),
            pltpu.VMEM((7 * FX, FY * SUB, LANE), jnp.float32),
            pltpu.VMEM((NX, NY * SUB, LANE), jnp.float32),
            pltpu.VMEM((NX, NY * SUB, LANE), jnp.float32),
            pltpu.VMEM((NX, NY * SUB, LANE), jnp.float32),
            pltpu.VMEM((NX, NY * SUB, LANE), jnp.float32),
            pltpu.VMEM((NX, NY * SUB, LANE), jnp.float32),
            pltpu.VMEM((3, SUB, LANE), jnp.float32),
            pltpu.VMEM((2, SUB, LANE), jnp.float32),
            pltpu.VMEM((4, 1, LANE), jnp.float32),
            pltpu.VMEM((4, most - 1, 1, LANE), jnp.float32),
            pltpu.SemaphoreType.DMA((3,)),
            pltpu.SemaphoreType.DMA((2, 2, NY)),
            pltpu.SemaphoreType.DMA((2, 2, NY)),
            pltpu.SemaphoreType.DMA((2, 2)),
            pltpu.SemaphoreType.DMA((2, 2)),
            pltpu.SemaphoreType.DMA((4,)),
            pltpu.SemaphoreType.DMA((4,)),
        ],
        compiler_params=pltpu.CompilerParams(collective_id=0, has_side_effects=True),
    )(initial_value, disturbance, jnp.asarray(coordinate_tables()))


def solution(mesh):
    placed = (P("gx", "gy", None), P("gx", "gy"))
    return jax.shard_map(
        functools.partial(body, mesh.shape["gx"], mesh.shape["gy"]),
        mesh=mesh,
        in_specs=placed,
        out_specs=P("gx", "gy", None),
        check_vma=False,
    )
```

```python
import functools
import math

import jax
import jax.numpy as jnp
import numpy as np
from jax import lax
from jax.experimental import pallas as pl
from jax.experimental.pallas import tpu as pltpu
from jax.sharding import PartitionSpec as P

HEADINGS = 16
SPEEDS = 16
TURNS = 4
LANES = HEADINGS * SPEEDS * TURNS

NX = 4
NY = 8
SUB = 8
LANE = 128
TILES = LANES // LANE
FX = NX + 6
FY = NY + 6

SCALE = 4.0
step_xy = 0.1
step_heading = 2.0 * math.pi / HEADINGS
accel = 0.5
torque = 0.3
turn_peak = 0.1 * (TURNS - 1) / 2.0
EPS_XY = 0.75e-6 * (SCALE * step_xy) ** 2
EPS_HEADING = 0.75e-6 * (SCALE * step_heading) ** 2
RADIUS = 0.01 * (SCALE * 12.0 * step_xy) ** 2

MESH = pl.DeviceIdType.MESH


def coordinate_tables():
    lanes = np.arange(LANES)
    heading = (-math.pi + ((lanes % HEADINGS) + 0.5) * step_heading).astype(np.float32)
    speed = (1.0 + 0.1 * (lanes // HEADINGS % SPEEDS)).astype(np.float32)
    vx = speed * np.cos(heading)
    vy = speed * np.sin(heading)
    return np.stack([vx, vy]).astype(np.float32).reshape(2, SUB, LANE)


def corrections(s1, s2, s3, x1, x2):
    a = s2 * s3
    b = s1 * s3
    c = s1 * s2
    r1 = a * a
    r2 = b * b
    r3 = c * c
    mid = r1 + r3 + 6.0 * r2
    den_right = mid + (r3 + r3)
    den_left = mid + (r1 + r1)
    y1 = r1 * x1
    y2 = r3 * x2
    both = y1 + y2
    both = both + both
    right = (both + y2) / den_right
    left = (both + y1) / den_left
    return right, left


def smooth_outer(inner, outer_sq, inner_sq, product):
    return (2.5 * inner_sq - 2.75 * product) + outer_sq


def line_slopes(cells, eps):
    n = len(cells) - 6
    diff = [b - a for a, b in zip(cells[:-1], cells[1:])]
    second = [b - a for a, b in zip(diff[:-1], diff[1:])]
    third = [b - a for a, b in zip(second[:-1], second[1:])]
    fourth = [b - a for a, b in zip(third[:-1], third[1:])]
    sq = [e * e for e in second]
    sq_eps = [q + eps for q in sq]
    sq_big = [2.5 * q for q in sq]
    product = [a * b for a, b in zip(second[:-1], second[1:])]
    prod_outer = [2.75 * q for q in product]
    prod_inner = [1.25 * q for q in product]
    rights, lefts = [], []
    for k in range(n + 1):
        s1 = (sq_big[k + 1] - prod_outer[k]) + sq_eps[k]
        s2 = (sq[k + 1] - prod_inner[k + 1]) + sq_eps[k + 2]
        s3 = (sq_big[k + 2] - prod_outer[k + 2]) + sq_eps[k + 3]
        right, left = corrections(s1, s2, s3, fourth[k], fourth[k + 1])
        rights.append(right)
        lefts.append(left)
    sums, gaps = [], []
    for i in range(n):
        right, left = rights[i], lefts[i + 1]
        central = 6.0 * (diff[i + 2] + diff[i + 3]) - (second[i + 3] - second[i + 1])
        sums.append(central + (left - right))
        gaps.append((left + right) - fourth[i + 1])
    return sums, gaps


def edge_correction(g, eps):
    s = g * g + eps
    return (3.0 * eps * eps) * g / (7.0 * (s * s) + 3.0 * eps * eps)


def turn_slopes(cells, eps):
    d0, d1, d2 = (b - a for a, b in zip(cells[:-1], cells[1:]))
    e1 = d1 - d0
    e2 = d2 - d1
    sq1, sq2, p12 = e1 * e1, e2 * e2, e1 * e2
    big1, big2 = 2.5 * sq1, 2.5 * sq2
    one1, one2 = sq1 + eps, sq2 + eps
    x0, x1, x2, x3 = e1, e2 - (e1 + e1), e1 - (e2 + e2), e2
    outer = 2.75 * p12
    right_edge = edge_correction(e1, eps)
    left_edge = edge_correction(e2, eps)
    r0, l0 = corrections(eps, one1, (big1 - outer) + one2, x0, x1)
    r1, l1 = corrections(big1 + eps, (sq1 - 1.25 * p12) + one2, big2 + eps, x1, x2)
    r2, l2 = corrections((big2 - outer) + one1, one2, eps, x2, x3)
    rights, lefts = (right_edge, r0, r1, r2), (l0, l1, l2, left_edge)
    centrals = (
        12.0 * d0 - e1,
        6.0 * (d0 + d1) - e2,
        6.0 * (d1 + d2) + e1,
        12.0 * d2 + e2,
    )
    sums = [c + (le - ri) for c, le, ri in zip(centrals, lefts, rights)]
    gaps = [(le + ri) - x for x, le, ri in zip((x0, x1, x2, x3), lefts, rights)]
    return sums, gaps


def lane_corrections(em, e, ep, epp, eps):
    tm, t, tp = e - em, ep - e, epp - ep
    sq, sqp = e * e, ep * ep
    sqp_eps = sqp + eps
    s1 = e * (2.5 * e - 2.75 * em) + (em * em + eps)
    s2 = e * (e - 1.25 * ep) + sqp_eps
    s3 = ep * (2.5 * ep - 2.75 * epp) + (epp * epp + eps)
    x1 = t - tm
    right, left = corrections(s1, s2, s3, x1, tp - t)
    return right, left, x1


def heading_slopes(f, lane):
    place = lane % HEADINGS

    def moved(v, by):
        near = pltpu.roll(v, (-by) % LANE, 1)
        wrapped = pltpu.roll(v, (HEADINGS - by if by > 0 else -HEADINGS - by) % LANE, 1)
        inside = place < HEADINGS - by if by > 0 else place >= -by
        return jnp.where(inside, near, wrapped)

    d = moved(f, 1) - f
    dm = moved(d, -1)
    e = d - dm
    em, ep, epp = moved(e, -1), moved(e, 1), moved(e, 2)
    right, left, x1 = lane_corrections(em, e, ep, epp, EPS_HEADING)
    right = moved(right, -1)
    return 6.0 * (d + dm) - (ep - em) + (left - right), (left + right) - x1


def speed_slopes(pair, lane):
    first = lane < HEADINGS
    last = lane >= LANE - HEADINGS

    def up(vs):
        r0, r1 = (pltpu.roll(v, LANE - HEADINGS, 1) for v in vs)
        return jnp.where(last, r1, r0), jnp.where(last, r0, r1)

    def down(vs):
        r0, r1 = (pltpu.roll(v, HEADINGS, 1) for v in vs)
        return jnp.where(first, r1, r0), jnp.where(first, r0, r1)

    d = [b - a for a, b in zip(pair, up(pair))]
    dm = list(down(d))
    d[1] = jnp.where(last, dm[1], d[1])
    dm[0] = jnp.where(first, d[0], dm[0])
    e = [a - b for a, b in zip(d, dm)]
    em = down(e)
    ep = up(e)
    epp = list(up(ep))
    epp[1] = jnp.where(last, 0.0, epp[1])
    out = [lane_corrections(em[k], e[k], ep[k], epp[k], EPS_XY) for k in range(2)]
    rights = list(down((out[0][0], out[1][0])))
    rights[0] = jnp.where(first, edge_correction(ep[0], EPS_XY), rights[0])
    sums = [
        6.0 * (d[k] + dm[k]) - (ep[k] - em[k]) + (out[k][1] - rights[k]) for k in range(2)
    ]
    gaps = [(out[k][1] + rights[k]) - out[k][2] for k in range(2)]
    return sums, gaps


def kernel(
    gx_count,
    gy_count,
    u_hbm,
    dist_hbm,
    coord_hbm,
    out_ref,
    u_ref,
    dist_ref,
    coord_ref,
    frame,
    flat,
    py,
    rates,
    alpha,
    peak,
    arsend,
    arrecv,
    load_sem,
    send_x_sem,
    recv_x_sem,
    send_y_sem,
    recv_y_sem,
    rate_send_sem,
    rate_recv_sem,
    rate_recv_x_sem,
    ar_send_sem,
    ar_recv_sem,
):
    gx = lax.axis_index("gx")
    gy = lax.axis_index("gy")

    loads = [
        pltpu.make_async_copy(src, dst, load_sem.at[k])
        for k, (src, dst) in enumerate(
            ((u_hbm, u_ref), (dist_hbm, dist_ref), (coord_hbm, coord_ref))
        )
    ]
    for load in loads:
        load.start()

    barrier = pltpu.get_barrier_semaphore()
    for count, axis in ((gx_count, 0), (gy_count, 1)):

        @pl.loop(0, count - 1)
        def _(i, count=count, axis=axis):
            k = lax.rem(i + count // 3, count - 1) + 1
            where = (lax.rem(gx + k, count), gy) if axis == 0 else (gx, lax.rem(gy + k, count))
            pl.semaphore_signal(barrier, inc=1, device_id=where, device_id_type=MESH)

    lane = lax.broadcasted_iota(jnp.int32, (SUB, LANE), 1)

    def cell(s, x, y):
        return (s * FX + x, pl.ds(y * SUB, SUB), slice(None))

    for load in loads:
        load.wait()

    for x in range(NX):
        for j in range(TILES):
            tile = u_ref[x, :, j * LANE : (j + 1) * LANE]
            frame[3 + x, pl.ds(3 * SUB + j, SUB, stride=SUB), :] = SCALE * tile

    def flat_pass(s):
        @pl.loop(0, NX)
        def _(x):
            row = s * FX + 3 + x
            tiles = [frame[row, pl.ds(3 * SUB + j, SUB, stride=SUB), :] for j in range(TILES)]
            parts = [None] * TILES
            for j in range(TILES):
                total, gap = heading_slopes(tiles[j], lane)
                rate = 0.1 * (j // 2 - (TURNS - 1) / 2.0)
                parts[j] = (turn_peak / (12.0 * step_heading)) * gap - (
                    rate / (12.0 * step_heading)
                ) * total
            for c in range(TURNS):
                sums, gaps = speed_slopes(tiles[2 * c : 2 * c + 2], lane)
                for k in range(2):
                    parts[2 * c + k] += (accel / (12.0 * step_xy)) * (gaps[k] - jnp.abs(sums[k]))
            for k in range(2):
                sums, gaps = turn_slopes(tiles[k::2], EPS_XY)
                for c in range(TURNS):
                    parts[2 * c + k] += (torque / (12.0 * step_xy)) * (gaps[c] - jnp.abs(sums[c]))
            for j in range(TILES):
                flat[x, pl.ds(j, SUB, stride=SUB), :] = parts[j]

    sends = (gx < gx_count - 1, gx > 0, gy < gy_count - 1, gy > 0)
    receives = (gx > 0, gx < gx_count - 1, gy > 0, gy < gy_count - 1)

    def halo_x(s, way, y):
        row = s * FX
        turn = lax.rem(s, 2)
        at = pl.ds((3 + y) * SUB, SUB)
        return pltpu.make_async_remote_copy(
            src_ref=frame.at[pl.ds(row + (4 if way == 0 else 3), 3), at],
            dst_ref=frame.at[pl.ds(row + (0 if way == 0 else 3 + NX), 3), at],
            send_sem=send_x_sem.at[turn, way],
            recv_sem=recv_x_sem.at[turn, way, y],
            device_id=(gx + 1, gy) if way == 0 else (gx - 1, gy),
            device_id_type=MESH,
        )

    def halo_y(s, way):
        rows = pl.ds(s * FX + 3, NX)
        turn = lax.rem(s, 2)
        return pltpu.make_async_remote_copy(
            src_ref=frame.at[rows, pl.ds((NY if way == 0 else 3) * SUB, 3 * SUB)],
            dst_ref=frame.at[rows, pl.ds((0 if way == 0 else 3 + NY) * SUB, 3 * SUB)],
            send_sem=send_y_sem.at[turn, way],
            recv_sem=recv_y_sem.at[turn, way],
            device_id=(gx, gy + 1) if way == 0 else (gx, gy - 1),
            device_id_type=MESH,
        )

    def column(i):
        return jnp.where(i < 3, i, jnp.where(i < 6, i + 2, i - 3))

    def send_column(s, y):
        for way in range(2):

            @pl.when(sends[way])
            def _(way=way):
                halo_x(s, way, y).start()

    def send_rows(s, i):
        @pl.when(jnp.logical_and(i == 2, sends[3]))
        def _():
            halo_y(s, 1).start()

        @pl.when(jnp.logical_and(i == 5, sends[2]))
        def _():
            halo_y(s, 0).start()

    def finish_sends(s):
        turn = lax.rem(s, 2)
        every = frame.at[pl.ds(0, 3), pl.ds(3 * SUB, NY * SUB)]
        for way in range(2):

            @pl.when(sends[way])
            def _(way=way):
                pltpu.make_async_remote_copy(
                    src_ref=every,
                    dst_ref=every,
                    send_sem=send_x_sem.at[turn, way],
                    recv_sem=recv_x_sem.at[turn, way, 0],
                    device_id=(gx, gy),
                    device_id_type=MESH,
                ).wait_send()

            @pl.when(sends[2 + way])
            def _(way=way):
                halo_y(s, way).wait_send()

    def rate_x(way, y):
        at = pl.ds((3 + y) * SUB, SUB)
        return pltpu.make_async_remote_copy(
            src_ref=rates.at[pl.ds(0, 3), pl.ds(4 if way == 0 else 3, 3), at],
            dst_ref=rates.at[pl.ds(0, 3), pl.ds(0 if way == 0 else 3 + NX, 3), at],
            send_sem=rate_send_sem.at[way],
            recv_sem=rate_recv_x_sem.at[way, y],
            device_id=(gx + 1, gy) if way == 0 else (gx - 1, gy),
            device_id_type=MESH,
        )

    def rate_y(way):
        rows = pl.ds(3, NX)
        return pltpu.make_async_remote_copy(
            src_ref=rates.at[pl.ds(0, 3), rows, pl.ds((NY if way == 0 else 3) * SUB, 3 * SUB)],
            dst_ref=rates.at[pl.ds(0, 3), rows, pl.ds((0 if way == 0 else 3 + NY) * SUB, 3 * SUB)],
            send_sem=rate_send_sem.at[2 + way],
            recv_sem=rate_recv_sem.at[way],
            device_id=(gx, gy + 1) if way == 0 else (gx, gy - 1),
            device_id_type=MESH,
        )

    def send_rates(i, y):
        for way in range(2):

            @pl.when(sends[way])
            def _(way=way):
                rate_x(way, y).start()

        @pl.when(jnp.logical_and(i == 2, sends[3]))
        def _():
            rate_y(1).start()

        @pl.when(jnp.logical_and(i == 5, sends[2]))
        def _():
            rate_y(0).start()

    def finish_rates():
        every = rates.at[pl.ds(0, 3), pl.ds(0, 3), pl.ds(3 * SUB, NY * SUB)]
        for way in range(2):

            @pl.when(sends[way])
            def _(way=way):
                pltpu.make_async_remote_copy(
                    src_ref=every,
                    dst_ref=every,
                    send_sem=rate_send_sem.at[way],
                    recv_sem=rate_recv_x_sem.at[way, 0],
                    device_id=(gx, gy),
                    device_id_type=MESH,
                ).wait_send()

            @pl.when(sends[2 + way])
            def _(way=way):
                rate_y(way).wait_send()

    def first_move(s, x, y):
        at = pl.ds(y * SUB, SUB)
        rate = rates[0, x, at, :] + (alpha[0] * rates[1, x, at, :] + alpha[1] * rates[2, x, at, :])
        frame[cell(s, x, y)] = frame[cell(s - 1, x, y)] + alpha[2] * rate

    def fill_ghosts(s):
        for low, outside in ((True, gx == 0), (False, gx == gx_count - 1)):

            @pl.when(outside)
            def _(low=low):
                end, inner, step = (3, 4, -1) if low else (2 + NX, 1 + NX, 1)

                @pl.loop(0, NY)
                def _(y):
                    edge = frame[cell(s, end, 3 + y)]
                    slope = edge - frame[cell(s, inner, 3 + y)]
                    for k in (1, 2, 3):
                        frame[cell(s, end + step * k, 3 + y)] = edge + float(k) * slope

        for low, outside in ((True, gy == 0), (False, gy == gy_count - 1)):

            @pl.when(outside)
            def _(low=low):
                end, inner, step = (3, 4, -1) if low else (2 + NY, 1 + NY, 1)

                @pl.loop(0, NX)
                def _(x):
                    edge = frame[cell(s, 3 + x, end)]
                    slope = edge - frame[cell(s, 3 + x, inner)]
                    for k in (1, 2, 3):
                        frame[cell(s, 3 + x, end + step * k)] = edge + float(k) * slope

    def second_pass(s, part):
        slot = jnp.where(part == 0, 2, 3)

        for way in range(2):

            @pl.when(jnp.logical_and(receives[2 + way], part != 1))
            def _(way=way):
                halo_y(s, way).wait_recv()

            @pl.when(jnp.logical_and(receives[2 + way], part == 1))
            def _(way=way):
                rate_y(way).wait_recv()

                @pl.loop(0, NX)
                def _(x):
                    for k in range(3):
                        first_move(s, 3 + x, k + (0 if way == 0 else 3 + NY))

        @pl.loop(0, NX)
        def _(x):
            sums, gaps = line_slopes([frame[cell(s, 3 + x, i)] for i in range(FY)], EPS_XY)
            for y in range(NY):
                py[x, pl.ds(y * SUB, SUB), :] = sums[y]
                rates[slot, 3 + x, pl.ds((3 + y) * SUB, SUB), :] = gaps[y]

    def first_slopes(s, y):
        sums, gaps = line_slopes([frame[cell(s, i, 3 + y)] for i in range(FX)], EPS_XY)
        vx = coord_ref[0]
        vy = coord_ref[1]
        top_x, top_y = peak[0], peak[1]
        moves = []
        for x in range(NX):
            at = (x, pl.ds(y * SUB, SUB), slice(None))
            bound = dist_ref[x, y]
            sx, sy = sums[x], py[at]
            square = sx * sx + sy * sy + RADIUS
            pull = bound * lax.rsqrt(square)
            top_x = jnp.maximum(top_x, jnp.abs(vx - pull * sx))
            top_y = jnp.maximum(top_y, jnp.abs(vy - pull * sy))
            moves.append(
                flat[at] + (1.0 / (12.0 * step_xy)) * ((pull * square) - (sx * vx + sy * vy))
            )
        peak[0] = top_x
        peak[1] = top_y
        return moves, gaps

    half = lane < LANE // 2

    def fold(v):
        for by in (4, 2, 1):
            v = jnp.maximum(v, pltpu.roll(v, by, 0))
        return jnp.maximum(v, pltpu.roll(v, LANE // 2, 1))

    def ar_copy(turn, phase, k):
        count = gy_count if phase == 0 else gx_count
        where = (gx, lax.rem(gy + k, count)) if phase == 0 else (lax.rem(gx + k, count), gy)
        return pltpu.make_async_remote_copy(
            src_ref=arsend.at[2 * turn + phase],
            dst_ref=arrecv.at[2 * turn + phase, k - 1],
            send_sem=ar_send_sem.at[2 * turn + phase],
            recv_sem=ar_recv_sem.at[2 * turn + phase],
            device_id=where,
            device_id_type=MESH,
        )

    def ar_start(turn, phase, row):
        arsend[2 * turn + phase] = row

        count = gy_count if phase == 0 else gx_count

        @pl.loop(0, count - 1)
        def _(i):
            ar_copy(turn, phase, lax.rem(i + count // 3, count - 1) + 1).start()

    def ar_finish(turn, phase):
        count = gy_count if phase == 0 else gx_count
        slot = 2 * turn + phase
        every = arrecv.at[slot, pl.ds(0, count - 1)]
        whole = pltpu.make_async_remote_copy(
            src_ref=every,
            dst_ref=every,
            send_sem=ar_send_sem.at[slot],
            recv_sem=ar_recv_sem.at[slot],
            device_id=(gx, gy),
            device_id_type=MESH,
        )
        whole.wait_send()
        whole.wait_recv()
        row = arsend[slot]
        for k in range(count - 1):
            row = jnp.maximum(row, arrecv[slot, k])
        return row

    def own_row():
        return jnp.where(half, fold(peak[0]), fold(peak[1]))[0:1]

    def set_alpha(row):
        row = jnp.broadcast_to(row, (SUB, LANE))
        ax = jnp.max(jnp.where(half, row, 0.0), axis=1, keepdims=True)
        ay = jnp.max(jnp.where(half, 0.0, row), axis=1, keepdims=True)
        ax = jnp.broadcast_to(ax, (SUB, LANE))
        ay = jnp.broadcast_to(ay, (SUB, LANE))
        total = ax / step_xy + ay / step_xy + turn_peak / step_heading
        alpha[0] = (1.0 / (12.0 * step_xy)) * ax
        alpha[1] = (1.0 / (12.0 * step_xy)) * ay
        alpha[2] = 0.75 / (total + accel / step_xy + torque / step_xy)

    peak[...] = jnp.zeros_like(peak)

    pl.semaphore_wait(barrier, gx_count + gy_count - 2)

    @pl.loop(0, NY)
    def _(i):
        send_column(0, column(i))
        send_rows(0, i)

    @pl.loop(0, 6)
    def _(s):
        part = lax.rem(s, 3)
        base = s - part

        flat_pass(s)
        fill_ghosts(s)
        second_pass(s, part)

        @pl.when(s == 3)
        def _():
            ar_start(1, 1, ar_finish(1, 0))

        @pl.when(part == 0)
        def _():
            @pl.loop(0, NY)
            def _(i):
                y = column(i)
                for way in range(2):

                    @pl.when(receives[way])
                    def _(way=way):
                        halo_x(s, way, y).wait_recv()

                moves, gaps = first_slopes(s, y)
                for x in range(NX):
                    rates[0, 3 + x, pl.ds((3 + y) * SUB, SUB), :] = moves[x]
                    rates[1, 3 + x, pl.ds((3 + y) * SUB, SUB), :] = gaps[x]
                send_rates(i, y)

            @pl.when(s == 0)
            def _():
                ar_start(0, 0, own_row())
                ar_start(0, 1, ar_finish(0, 0))
                set_alpha(ar_finish(0, 1))
                peak[...] = jnp.zeros_like(peak)

            @pl.when(s == 3)
            def _():
                set_alpha(ar_finish(1, 1))

            @pl.loop(0, NY)
            def _(y):
                for x in range(NX):
                    first_move(s + 1, 3 + x, 3 + y)

            finish_sends(s)

        @pl.when(part > 0)
        def _():
            keep = jnp.where(part == 1, 0.75, 1.0 / 3.0)
            take = jnp.where(part == 1, 0.25, 2.0 / 3.0)

            @pl.loop(0, NY)
            def _(i):
                y = column(i)
                for way in range(2):

                    @pl.when(jnp.logical_and(receives[way], part == 2))
                    def _(way=way):
                        halo_x(s, way, y).wait_recv()

                    @pl.when(jnp.logical_and(receives[way], part == 1))
                    def _(way=way):
                        rate_x(way, y).wait_recv()
                        for k in range(3):
                            first_move(s, k + (0 if way == 0 else 3 + NX), 3 + y)

                moves, gaps = first_slopes(s, y)
                ax, ay, dt = alpha[0], alpha[1], alpha[2]
                for x in range(NX):
                    gap_y = rates[3, 3 + x, pl.ds((3 + y) * SUB, SUB), :]
                    rate = moves[x] + (ax * gaps[x] + ay * gap_y)
                    moved = frame[cell(s, 3 + x, 3 + y)] + dt * rate
                    frame[cell(s + 1, 3 + x, 3 + y)] = (
                        keep * frame[cell(base, 3 + x, 3 + y)] + take * moved
                    )

                @pl.when(s < 5)
                def _():
                    send_column(s + 1, y)
                    send_rows(s + 1, i)

            @pl.when(part == 1)
            def _():
                finish_rates()

            @pl.when(part == 2)
            def _():
                finish_sends(s)

        @pl.when(s == 2)
        def _():
            ar_start(1, 0, own_row())

    for x in range(NX):
        for j in range(TILES):
            tile = frame[6 * FX + 3 + x, pl.ds(3 * SUB + j, SUB, stride=SUB), :]
            out_ref[x, :, j * LANE : (j + 1) * LANE] = (1.0 / SCALE) * tile


def body(gx_count, gy_count, initial_value, disturbance):
    most = max(gx_count, gy_count)
    return pl.pallas_call(
        functools.partial(kernel, gx_count, gy_count),
        out_shape=pltpu.VMEM((NX, NY, LANES), jnp.float32),
        in_specs=[pl.BlockSpec(memory_space=pl.ANY)] * 3,
        out_specs=pl.BlockSpec(memory_space=pltpu.VMEM),
        scratch_shapes=[
            pltpu.VMEM((NX, NY, LANES), jnp.float32),
            pltpu.SMEM((NX, NY), jnp.float32),
            pltpu.VMEM((2, SUB, LANE), jnp.float32),
            pltpu.VMEM((7 * FX, FY * SUB, LANE), jnp.float32),
            pltpu.VMEM((NX, NY * SUB, LANE), jnp.float32),
            pltpu.VMEM((NX, NY * SUB, LANE), jnp.float32),
            pltpu.VMEM((4, FX, FY * SUB, LANE), jnp.float32),
            pltpu.VMEM((3, SUB, LANE), jnp.float32),
            pltpu.VMEM((2, SUB, LANE), jnp.float32),
            pltpu.VMEM((4, 1, LANE), jnp.float32),
            pltpu.VMEM((4, most - 1, 1, LANE), jnp.float32),
            pltpu.SemaphoreType.DMA((3,)),
            pltpu.SemaphoreType.DMA((2, 2)),
            pltpu.SemaphoreType.DMA((2, 2, NY)),
            pltpu.SemaphoreType.DMA((2, 2)),
            pltpu.SemaphoreType.DMA((2, 2)),
            pltpu.SemaphoreType.DMA((4,)),
            pltpu.SemaphoreType.DMA((2,)),
            pltpu.SemaphoreType.DMA((2, NY)),
            pltpu.SemaphoreType.DMA((4,)),
            pltpu.SemaphoreType.DMA((4,)),
        ],
        compiler_params=pltpu.CompilerParams(collective_id=0, has_side_effects=True),
    )(initial_value, disturbance, jnp.asarray(coordinate_tables()))


def solution(mesh):
    placed = (P("gx", "gy", None), P("gx", "gy"))
    return jax.shard_map(
        functools.partial(body, mesh.shape["gx"], mesh.shape["gy"]),
        mesh=mesh,
        in_specs=placed,
        out_specs=P("gx", "gy", None),
        check_vma=False,
    )
```

```python
import functools
import math

import jax
import jax.numpy as jnp
import numpy as np
from jax import lax
from jax.experimental import pallas as pl
from jax.experimental.pallas import tpu as pltpu
from jax.sharding import PartitionSpec as P

HEADINGS = 16
SPEEDS = 16
TURNS = 4
LANES = HEADINGS * SPEEDS * TURNS

NX = 4
NY = 8
SUB = 8
LANE = 128
TILES = LANES // LANE
PITCH = NY + 1
FX = NX + 6
FY = NY + 6

SCALE = 4.0
step_xy = 0.1
step_heading = 2.0 * math.pi / HEADINGS
accel = 0.5
torque = 0.3
turn_peak = 0.1 * (TURNS - 1) / 2.0
EPS_XY = 0.75e-6 * (SCALE * step_xy) ** 2
EPS_HEADING = 0.75e-6 * (SCALE * step_heading) ** 2
RADIUS = 0.01 * (SCALE * 12.0 * step_xy) ** 2

MESH = pl.DeviceIdType.MESH


def coordinate_tables():
    lanes = np.arange(LANES)
    heading = (-math.pi + ((lanes % HEADINGS) + 0.5) * step_heading).astype(np.float32)
    speed = (1.0 + 0.1 * (lanes // HEADINGS % SPEEDS)).astype(np.float32)
    vx = speed * np.cos(heading)
    vy = speed * np.sin(heading)
    return np.stack([vx, vy]).astype(np.float32).reshape(2, SUB, LANE)


def corrections(s1, s2, s3, x1, x2):
    a = s2 * s3
    b = s1 * s3
    c = s1 * s2
    r1 = a * a
    r2 = b * b
    r3 = c * c
    mid = r1 + r3 + 6.0 * r2
    den_right = mid + (r3 + r3)
    den_left = mid + (r1 + r1)
    y1 = r1 * x1
    y2 = r3 * x2
    both = y1 + y2
    both = both + both
    right = (both + y2) / den_right
    left = (both + y1) / den_left
    return right, left


def smooth_outer(inner, outer_sq, inner_sq, product):
    return (2.5 * inner_sq - 2.75 * product) + outer_sq


def line_slopes(cells, eps):
    n = len(cells) - 6
    diff = [b - a for a, b in zip(cells[:-1], cells[1:])]
    second = [b - a for a, b in zip(diff[:-1], diff[1:])]
    third = [b - a for a, b in zip(second[:-1], second[1:])]
    fourth = [b - a for a, b in zip(third[:-1], third[1:])]
    sq = [e * e for e in second]
    sq_eps = [q + eps for q in sq]
    sq_big = [2.5 * q for q in sq]
    product = [a * b for a, b in zip(second[:-1], second[1:])]
    prod_outer = [2.75 * q for q in product]
    prod_inner = [1.25 * q for q in product]
    rights, lefts = [], []
    for k in range(n + 1):
        s1 = (sq_big[k + 1] - prod_outer[k]) + sq_eps[k]
        s2 = (sq[k + 1] - prod_inner[k + 1]) + sq_eps[k + 2]
        s3 = (sq_big[k + 2] - prod_outer[k + 2]) + sq_eps[k + 3]
        right, left = corrections(s1, s2, s3, fourth[k], fourth[k + 1])
        rights.append(right)
        lefts.append(left)
    sums, gaps = [], []
    for i in range(n):
        right, left = rights[i], lefts[i + 1]
        central = 6.0 * (diff[i + 2] + diff[i + 3]) - (second[i + 3] - second[i + 1])
        sums.append(central + (left - right))
        gaps.append((left + right) - fourth[i + 1])
    return sums, gaps


def edge_correction(g, eps):
    s = g * g + eps
    return (3.0 * eps * eps) * g / (7.0 * (s * s) + 3.0 * eps * eps)


def turn_slopes(cells, eps):
    d0, d1, d2 = (b - a for a, b in zip(cells[:-1], cells[1:]))
    e1 = d1 - d0
    e2 = d2 - d1
    sq1, sq2, p12 = e1 * e1, e2 * e2, e1 * e2
    big1, big2 = 2.5 * sq1, 2.5 * sq2
    one1, one2 = sq1 + eps, sq2 + eps
    x0, x1, x2, x3 = e1, e2 - (e1 + e1), e1 - (e2 + e2), e2
    outer = 2.75 * p12
    right_edge = edge_correction(e1, eps)
    left_edge = edge_correction(e2, eps)
    r0, l0 = corrections(eps, one1, (big1 - outer) + one2, x0, x1)
    r1, l1 = corrections(big1 + eps, (sq1 - 1.25 * p12) + one2, big2 + eps, x1, x2)
    r2, l2 = corrections((big2 - outer) + one1, one2, eps, x2, x3)
    rights, lefts = (right_edge, r0, r1, r2), (l0, l1, l2, left_edge)
    centrals = (
        12.0 * d0 - e1,
        6.0 * (d0 + d1) - e2,
        6.0 * (d1 + d2) + e1,
        12.0 * d2 + e2,
    )
    sums = [c + (le - ri) for c, le, ri in zip(centrals, lefts, rights)]
    gaps = [(le + ri) - x for x, le, ri in zip((x0, x1, x2, x3), lefts, rights)]
    return sums, gaps


def lane_corrections(em, e, ep, epp, eps):
    tm, t, tp = e - em, ep - e, epp - ep
    sq, sqp = e * e, ep * ep
    sqp_eps = sqp + eps
    s1 = e * (2.5 * e - 2.75 * em) + (em * em + eps)
    s2 = e * (e - 1.25 * ep) + sqp_eps
    s3 = ep * (2.5 * ep - 2.75 * epp) + (epp * epp + eps)
    x1 = t - tm
    right, left = corrections(s1, s2, s3, x1, tp - t)
    return right, left, x1


def heading_slopes(f, lane):
    place = lane % HEADINGS

    def moved(v, by):
        near = pltpu.roll(v, (-by) % LANE, 1)
        wrapped = pltpu.roll(v, (HEADINGS - by if by > 0 else -HEADINGS - by) % LANE, 1)
        inside = place < HEADINGS - by if by > 0 else place >= -by
        return jnp.where(inside, near, wrapped)

    d = moved(f, 1) - f
    dm = moved(d, -1)
    e = d - dm
    em, ep, epp = moved(e, -1), moved(e, 1), moved(e, 2)
    right, left, x1 = lane_corrections(em, e, ep, epp, EPS_HEADING)
    right = moved(right, -1)
    return 6.0 * (d + dm) - (ep - em) + (left - right), (left + right) - x1


def speed_slopes(pair, lane):
    first = lane < HEADINGS
    last = lane >= LANE - HEADINGS

    def up(vs):
        r0, r1 = (pltpu.roll(v, LANE - HEADINGS, 1) for v in vs)
        return jnp.where(last, r1, r0), jnp.where(last, r0, r1)

    def down(vs):
        r0, r1 = (pltpu.roll(v, HEADINGS, 1) for v in vs)
        return jnp.where(first, r1, r0), jnp.where(first, r0, r1)

    d = [b - a for a, b in zip(pair, up(pair))]
    dm = list(down(d))
    d[1] = jnp.where(last, dm[1], d[1])
    dm[0] = jnp.where(first, d[0], dm[0])
    e = [a - b for a, b in zip(d, dm)]
    em = down(e)
    ep = up(e)
    epp = list(up(ep))
    epp[1] = jnp.where(last, 0.0, epp[1])
    out = [lane_corrections(em[k], e[k], ep[k], epp[k], EPS_XY) for k in range(2)]
    rights = list(down((out[0][0], out[1][0])))
    rights[0] = jnp.where(first, edge_correction(ep[0], EPS_XY), rights[0])
    sums = [
        6.0 * (d[k] + dm[k]) - (ep[k] - em[k]) + (out[k][1] - rights[k]) for k in range(2)
    ]
    gaps = [(out[k][1] + rights[k]) - out[k][2] for k in range(2)]
    return sums, gaps


def kernel(
    gx_count,
    gy_count,
    u_hbm,
    dist_hbm,
    coord_hbm,
    out_ref,
    u_ref,
    dist_ref,
    coord_ref,
    frame,
    turned,
    flat,
    py,
    rates,
    alpha,
    peak,
    arsend,
    arrecv,
    load_sem,
    send_x_sem,
    recv_x_sem,
    send_y_sem,
    recv_y_sem,
    rate_send_sem,
    rate_recv_sem,
    rate_recv_x_sem,
    ar_send_sem,
    ar_recv_sem,
):
    gx = lax.axis_index("gx")
    gy = lax.axis_index("gy")

    loads = [
        pltpu.make_async_copy(src, dst, load_sem.at[k])
        for k, (src, dst) in enumerate(
            ((u_hbm, u_ref), (dist_hbm, dist_ref), (coord_hbm, coord_ref))
        )
    ]
    for load in loads:
        load.start()

    barrier = pltpu.get_barrier_semaphore()
    for count, axis in ((gx_count, 0), (gy_count, 1)):

        @pl.loop(0, count - 1)
        def _(i, count=count, axis=axis):
            k = i + count // 3 + 1
            k = jnp.where(k < count, k, k - count + 1)
            where = (lax.rem(gx + k, count), gy) if axis == 0 else (gx, lax.rem(gy + k, count))
            pl.semaphore_signal(barrier, inc=1, device_id=where, device_id_type=MESH)

    lane = lax.broadcasted_iota(jnp.int32, (SUB, LANE), 1)

    def cell(s, x, y):
        return (s * FX + x, pl.ds(y * SUB, SUB), slice(None))

    for load in loads:
        load.wait()

    for x in range(NX):
        for j in range(TILES):
            tile = u_ref[x, :, j * LANE : (j + 1) * LANE]
            turned[x, pl.ds(j * PITCH, NY), :] = SCALE * tile
    for x in range(NX):
        for y in range(NY):
            frame[cell(0, 3 + x, 3 + y)] = turned[x, pl.ds(y, SUB, stride=PITCH), :]

    def flat_pass():
        @pl.loop(0, NX)
        def _(x):
            tiles = [turned[x, pl.ds(j * PITCH, NY), :] for j in range(TILES)]
            parts = [None] * TILES
            for j in range(TILES):
                total, gap = heading_slopes(tiles[j], lane)
                rate = 0.1 * (j // 2 - (TURNS - 1) / 2.0)
                parts[j] = (turn_peak / (12.0 * step_heading)) * gap - (
                    rate / (12.0 * step_heading)
                ) * total
            for c in range(TURNS):
                sums, gaps = speed_slopes(tiles[2 * c : 2 * c + 2], lane)
                for k in range(2):
                    parts[2 * c + k] += (accel / (12.0 * step_xy)) * (gaps[k] - jnp.abs(sums[k]))
            for k in range(2):
                sums, gaps = turn_slopes(tiles[k::2], EPS_XY)
                for c in range(TURNS):
                    parts[2 * c + k] += (torque / (12.0 * step_xy)) * (gaps[c] - jnp.abs(sums[c]))
            for j in range(TILES):
                flat[x, pl.ds(j * PITCH, NY), :] = parts[j]

    sends = (gx < gx_count - 1, gx > 0, gy < gy_count - 1, gy > 0)
    receives = (gx > 0, gx < gx_count - 1, gy > 0, gy < gy_count - 1)

    def halo_x(s, way, y):
        row = s * FX
        turn = lax.rem(s, 2)
        at = pl.ds((3 + y) * SUB, SUB)
        return pltpu.make_async_remote_copy(
            src_ref=frame.at[pl.ds(row + (4 if way == 0 else 3), 3), at],
            dst_ref=frame.at[pl.ds(row + (0 if way == 0 else 3 + NX), 3), at],
            send_sem=send_x_sem.at[turn, way],
            recv_sem=recv_x_sem.at[turn, way, y],
            device_id=(gx + 1, gy) if way == 0 else (gx - 1, gy),
            device_id_type=MESH,
        )

    def halo_y(s, way):
        rows = pl.ds(s * FX + 3, NX)
        turn = lax.rem(s, 2)
        return pltpu.make_async_remote_copy(
            src_ref=frame.at[rows, pl.ds((NY if way == 0 else 3) * SUB, 3 * SUB)],
            dst_ref=frame.at[rows, pl.ds((0 if way == 0 else 3 + NY) * SUB, 3 * SUB)],
            send_sem=send_y_sem.at[turn, way],
            recv_sem=recv_y_sem.at[turn, way],
            device_id=(gx, gy + 1) if way == 0 else (gx, gy - 1),
            device_id_type=MESH,
        )

    def column(i):
        return jnp.where(i < 3, i, jnp.where(i < 6, i + 2, i - 3))

    def send_column(s, y, when=True):
        for way in range(2):

            @pl.when(jnp.logical_and(sends[way], when))
            def _(way=way):
                halo_x(s, way, y).start()

    def send_rows(s, i, when=True):
        for way, last in ((1, 2), (0, 5)):

            @pl.when(jnp.logical_and(jnp.logical_and(i == last, sends[2 + way]), when))
            def _(way=way):
                halo_y(s, way).start()

    def finish_sends(s):
        turn = lax.rem(s, 2)
        every = frame.at[pl.ds(0, 3), pl.ds(3 * SUB, NY * SUB)]
        for way in range(2):

            @pl.when(sends[way])
            def _(way=way):
                pltpu.make_async_remote_copy(
                    src_ref=every,
                    dst_ref=every,
                    send_sem=send_x_sem.at[turn, way],
                    recv_sem=recv_x_sem.at[turn, way, 0],
                    device_id=(gx, gy),
                    device_id_type=MESH,
                ).wait_send()

            @pl.when(sends[2 + way])
            def _(way=way):
                halo_y(s, way).wait_send()

    def rate_x(way, y):
        at = pl.ds((3 + y) * SUB, SUB)
        return pltpu.make_async_remote_copy(
            src_ref=rates.at[pl.ds(0, 3), pl.ds(4 if way == 0 else 3, 3), at],
            dst_ref=rates.at[pl.ds(0, 3), pl.ds(0 if way == 0 else 3 + NX, 3), at],
            send_sem=rate_send_sem.at[way],
            recv_sem=rate_recv_x_sem.at[way, y],
            device_id=(gx + 1, gy) if way == 0 else (gx - 1, gy),
            device_id_type=MESH,
        )

    def rate_y(way):
        rows = pl.ds(3, NX)
        return pltpu.make_async_remote_copy(
            src_ref=rates.at[pl.ds(0, 3), rows, pl.ds((NY if way == 0 else 3) * SUB, 3 * SUB)],
            dst_ref=rates.at[pl.ds(0, 3), rows, pl.ds((0 if way == 0 else 3 + NY) * SUB, 3 * SUB)],
            send_sem=rate_send_sem.at[2 + way],
            recv_sem=rate_recv_sem.at[way],
            device_id=(gx, gy + 1) if way == 0 else (gx, gy - 1),
            device_id_type=MESH,
        )

    def send_rates(i, y):
        for way in range(2):

            @pl.when(sends[way])
            def _(way=way):
                rate_x(way, y).start()

        @pl.when(jnp.logical_and(i == 2, sends[3]))
        def _():
            rate_y(1).start()

        @pl.when(jnp.logical_and(i == 5, sends[2]))
        def _():
            rate_y(0).start()

    def finish_rates():
        every = rates.at[pl.ds(0, 3), pl.ds(0, 3), pl.ds(3 * SUB, NY * SUB)]
        for way in range(2):

            @pl.when(sends[way])
            def _(way=way):
                pltpu.make_async_remote_copy(
                    src_ref=every,
                    dst_ref=every,
                    send_sem=rate_send_sem.at[way],
                    recv_sem=rate_recv_x_sem.at[way, 0],
                    device_id=(gx, gy),
                    device_id_type=MESH,
                ).wait_send()

            @pl.when(sends[2 + way])
            def _(way=way):
                rate_y(way).wait_send()

    def first_moved(s, x, y):
        at = pl.ds(y * SUB, SUB)
        rate = rates[0, x, at, :] + (alpha[0] * rates[1, x, at, :] + alpha[1] * rates[2, x, at, :])
        return frame[cell(s - 1, x, y)] + alpha[2] * rate

    def first_move(s, x, y):
        frame[cell(s, x, y)] = first_moved(s, x, y)

    def fill_ghosts(s):
        for low, outside in ((True, gx == 0), (False, gx == gx_count - 1)):

            @pl.when(outside)
            def _(low=low):
                end, inner, step = (3, 4, -1) if low else (2 + NX, 1 + NX, 1)

                @pl.loop(0, NY)
                def _(y):
                    edge = frame[cell(s, end, 3 + y)]
                    slope = edge - frame[cell(s, inner, 3 + y)]
                    for k in (1, 2, 3):
                        frame[cell(s, end + step * k, 3 + y)] = edge + float(k) * slope

        for low, outside in ((True, gy == 0), (False, gy == gy_count - 1)):

            @pl.when(outside)
            def _(low=low):
                end, inner, step = (3, 4, -1) if low else (2 + NY, 1 + NY, 1)

                @pl.loop(0, NX)
                def _(x):
                    edge = frame[cell(s, 3 + x, end)]
                    slope = edge - frame[cell(s, 3 + x, inner)]
                    for k in (1, 2, 3):
                        frame[cell(s, 3 + x, end + step * k)] = edge + float(k) * slope

    def second_pass(s, third):
        slot = jnp.where(third == 0, 2, 3)

        for way in range(2):

            @pl.when(jnp.logical_and(receives[2 + way], third != 1))
            def _(way=way):
                halo_y(s, way).wait_recv()

            @pl.when(jnp.logical_and(receives[2 + way], third == 1))
            def _(way=way):
                rate_y(way).wait_recv()

                @pl.loop(0, NX)
                def _(x):
                    for k in range(3):
                        first_move(s, 3 + x, k + (0 if way == 0 else 3 + NY))

        @pl.loop(0, NX)
        def _(x):
            sums, gaps = line_slopes([frame[cell(s, 3 + x, i)] for i in range(FY)], EPS_XY)
            for y in range(NY):
                py[x, pl.ds(y * SUB, SUB), :] = sums[y]
                rates[slot, 3 + x, pl.ds((3 + y) * SUB, SUB), :] = gaps[y]

    def first_slopes(s, y):
        sums, gaps = line_slopes([frame[cell(s, i, 3 + y)] for i in range(FX)], EPS_XY)
        vx = coord_ref[0]
        vy = coord_ref[1]
        top_x, top_y = peak[0], peak[1]
        moves = []
        for x in range(NX):
            at = (x, pl.ds(y * SUB, SUB), slice(None))
            bound = dist_ref[x, y]
            sx, sy = sums[x], py[at]
            square = sx * sx + sy * sy + RADIUS
            pull = bound * lax.rsqrt(square)
            top_x = jnp.maximum(top_x, jnp.abs(vx - pull * sx))
            top_y = jnp.maximum(top_y, jnp.abs(vy - pull * sy))
            moves.append(
                flat[x, pl.ds(y, SUB, stride=PITCH), :] + (1.0 / (12.0 * step_xy)) * ((pull * square) - (sx * vx + sy * vy))
            )
        peak[0] = top_x
        peak[1] = top_y
        return moves, gaps

    half = lane < LANE // 2

    def fold(v):
        for by in (4, 2, 1):
            v = jnp.maximum(v, pltpu.roll(v, by, 0))
        return jnp.maximum(v, pltpu.roll(v, LANE // 2, 1))

    def ar_copy(turn, phase, k):
        count = gy_count if phase == 1 else gx_count
        where = (gx, lax.rem(gy + k, count)) if phase == 1 else (lax.rem(gx + k, count), gy)
        return pltpu.make_async_remote_copy(
            src_ref=arsend.at[2 * turn + phase],
            dst_ref=arrecv.at[2 * turn + phase, k - 1],
            send_sem=ar_send_sem.at[2 * turn + phase],
            recv_sem=ar_recv_sem.at[2 * turn + phase],
            device_id=where,
            device_id_type=MESH,
        )

    def ar_start(turn, phase, row):
        arsend[2 * turn + phase] = row

        count = gy_count if phase == 1 else gx_count

        @pl.loop(0, count - 1)
        def _(i):
            k = i + count // 3 + 1
            ar_copy(turn, phase, jnp.where(k < count, k, k - count + 1)).start()

    def ar_finish(turn, phase):
        count = gy_count if phase == 1 else gx_count
        slot = 2 * turn + phase
        every = arrecv.at[slot, pl.ds(0, count - 1)]
        whole = pltpu.make_async_remote_copy(
            src_ref=every,
            dst_ref=every,
            send_sem=ar_send_sem.at[slot],
            recv_sem=ar_recv_sem.at[slot],
            device_id=(gx, gy),
            device_id_type=MESH,
        )
        whole.wait_send()
        whole.wait_recv()
        row = arsend[slot]
        for k in range(count - 1):
            row = jnp.maximum(row, arrecv[slot, k])
        return row

    def own_row():
        return jnp.where(half, fold(peak[0]), fold(peak[1]))[0:1]

    def set_alpha(row):
        row = jnp.broadcast_to(row, (SUB, LANE))
        ax = jnp.max(jnp.where(half, row, 0.0), axis=1, keepdims=True)
        ay = jnp.max(jnp.where(half, 0.0, row), axis=1, keepdims=True)
        ax = jnp.broadcast_to(ax, (SUB, LANE))
        ay = jnp.broadcast_to(ay, (SUB, LANE))
        total = ax / step_xy + ay / step_xy + turn_peak / step_heading
        alpha[0] = (1.0 / (12.0 * step_xy)) * ax
        alpha[1] = (1.0 / (12.0 * step_xy)) * ay
        alpha[2] = 0.75 / (total + accel / step_xy + torque / step_xy)

    peak[...] = jnp.zeros_like(peak)

    pl.semaphore_wait(barrier, gx_count + gy_count - 2)

    @pl.loop(0, NY)
    def _(i):
        send_column(0, column(i))
        send_rows(0, i)

    @pl.loop(0, 6)
    def _(s):
        third = lax.rem(s, 3)
        base = s - third

        flat_pass()
        fill_ghosts(s)
        second_pass(s, third)

        @pl.when(third == 0)
        def _():
            @pl.loop(0, NY)
            def _(i):
                y = column(i)
                for way in range(2):

                    @pl.when(receives[way])
                    def _(way=way):
                        halo_x(s, way, y).wait_recv()

                moves, gaps = first_slopes(s, y)
                for x in range(NX):
                    rates[0, 3 + x, pl.ds((3 + y) * SUB, SUB), :] = moves[x]
                    rates[1, 3 + x, pl.ds((3 + y) * SUB, SUB), :] = gaps[x]

                @pl.when(jnp.logical_and(s == 3, i < 3))
                def _():
                    send_rates(i, y)

            @pl.when(s == 0)
            def _():
                ar_start(0, 0, own_row())

                @pl.loop(0, NY)
                def _(i):
                    send_rates(i, column(i))

                ar_start(0, 1, ar_finish(0, 0))
                set_alpha(ar_finish(0, 1))
                peak[...] = jnp.zeros_like(peak)

            @pl.when(s == 3)
            def _():
                ar_start(1, 1, ar_finish(1, 0))

                @pl.loop(3, NY)
                def _(i):
                    send_rates(i, column(i))

                set_alpha(ar_finish(1, 1))

            @pl.loop(0, NY)
            def _(y):
                for x in range(NX):
                    following = first_moved(s + 1, 3 + x, 3 + y)
                    frame[cell(s + 1, 3 + x, 3 + y)] = following
                    turned[x, pl.ds(y, SUB, stride=PITCH), :] = following

            finish_sends(s)

        def advance(y, keep, take):
            moves, gaps = first_slopes(s, y)
            ax, ay, dt = alpha[0], alpha[1], alpha[2]
            for x in range(NX):
                gap_y = rates[3, 3 + x, pl.ds((3 + y) * SUB, SUB), :]
                rate = moves[x] + (ax * gaps[x] + ay * gap_y)
                moved = frame[cell(s, 3 + x, 3 + y)] + dt * rate
                following = keep * frame[cell(base, 3 + x, 3 + y)] + take * moved
                frame[cell(s + 1, 3 + x, 3 + y)] = following
                turned[x, pl.ds(y, SUB, stride=PITCH), :] = following

        @pl.when(third == 1)
        def _():
            @pl.loop(0, NY)
            def _(i):
                y = column(i)
                for way in range(2):

                    @pl.when(receives[way])
                    def _(way=way):
                        rate_x(way, y).wait_recv()

                for way in range(2):
                    for k in range(3):
                        x = k + (0 if way == 0 else 3 + NX)
                        frame[cell(s, x, 3 + y)] = jnp.where(
                            receives[way], first_moved(s, x, 3 + y), frame[cell(s, x, 3 + y)]
                        )
                advance(y, 0.75, 0.25)
                send_column(s + 1, y)
                send_rows(s + 1, i)

            finish_rates()

        @pl.when(third == 2)
        def _():
            @pl.loop(0, NY)
            def _(i):
                y = column(i)
                for way in range(2):

                    @pl.when(receives[way])
                    def _(way=way):
                        halo_x(s, way, y).wait_recv()

                advance(y, 1.0 / 3.0, 2.0 / 3.0)
                send_column(s + 1, y, s < 5)
                send_rows(s + 1, i, s < 5)

            finish_sends(s)

        @pl.when(s == 2)
        def _():
            ar_start(1, 0, own_row())

    for x in range(NX):
        for j in range(TILES):
            tile = turned[x, pl.ds(j * PITCH, NY), :]
            out_ref[x, :, j * LANE : (j + 1) * LANE] = (1.0 / SCALE) * tile


def body(gx_count, gy_count, initial_value, disturbance):
    most = max(gx_count, gy_count)
    return pl.pallas_call(
        functools.partial(kernel, gx_count, gy_count),
        out_shape=pltpu.VMEM((NX, NY, LANES), jnp.float32),
        in_specs=[pl.BlockSpec(memory_space=pl.ANY)] * 3,
        out_specs=pl.BlockSpec(memory_space=pltpu.VMEM),
        scratch_shapes=[
            pltpu.VMEM((NX, NY, LANES), jnp.float32),
            pltpu.SMEM((NX, NY), jnp.float32),
            pltpu.VMEM((2, SUB, LANE), jnp.float32),
            pltpu.VMEM((7 * FX, FY * SUB, LANE), jnp.float32),
            pltpu.VMEM((NX, TILES * PITCH, LANE), jnp.float32),
            pltpu.VMEM((NX, TILES * PITCH, LANE), jnp.float32),
            pltpu.VMEM((NX, NY * SUB, LANE), jnp.float32),
            pltpu.VMEM((4, FX, FY * SUB, LANE), jnp.float32),
            pltpu.VMEM((3, SUB, LANE), jnp.float32),
            pltpu.VMEM((2, SUB, LANE), jnp.float32),
            pltpu.VMEM((4, 1, LANE), jnp.float32),
            pltpu.VMEM((4, most - 1, 1, LANE), jnp.float32),
            pltpu.SemaphoreType.DMA((3,)),
            pltpu.SemaphoreType.DMA((2, 2)),
            pltpu.SemaphoreType.DMA((2, 2, NY)),
            pltpu.SemaphoreType.DMA((2, 2)),
            pltpu.SemaphoreType.DMA((2, 2)),
            pltpu.SemaphoreType.DMA((4,)),
            pltpu.SemaphoreType.DMA((2,)),
            pltpu.SemaphoreType.DMA((2, NY)),
            pltpu.SemaphoreType.DMA((4,)),
            pltpu.SemaphoreType.DMA((4,)),
        ],
        compiler_params=pltpu.CompilerParams(collective_id=0, has_side_effects=True),
    )(initial_value, disturbance, jnp.asarray(coordinate_tables()))


def solution(mesh):
    placed = (P("gx", "gy", None), P("gx", "gy"))
    return jax.shard_map(
        functools.partial(body, mesh.shape["gx"], mesh.shape["gy"]),
        mesh=mesh,
        in_specs=placed,
        out_specs=P("gx", "gy", None),
        check_vma=False,
    )
```

```python
import functools
import math

import jax
import jax.numpy as jnp
import numpy as np
from jax import lax
from jax.experimental import pallas as pl
from jax.experimental.pallas import tpu as pltpu
from jax.sharding import PartitionSpec as P

HEADINGS = 16
SPEEDS = 16
TURNS = 4
LANES = HEADINGS * SPEEDS * TURNS

NX = 4
NY = 8
SUB = 8
LANE = 128
TILES = LANES // LANE
PITCH = NY + 1
FX = NX + 6
FY = NY + 6

SCALE = 4.0
step_xy = 0.1
step_heading = 2.0 * math.pi / HEADINGS
accel = 0.5
torque = 0.3
turn_peak = 0.1 * (TURNS - 1) / 2.0
EPS_XY = 0.75e-6 * (SCALE * step_xy) ** 2
EPS_HEADING = 0.75e-6 * (SCALE * step_heading) ** 2
RADIUS = 0.01 * (SCALE * 12.0 * step_xy) ** 2

MESH = pl.DeviceIdType.MESH


def coordinate_tables():
    lanes = np.arange(LANES)
    heading = (-math.pi + ((lanes % HEADINGS) + 0.5) * step_heading).astype(np.float32)
    speed = (1.0 + 0.1 * (lanes // HEADINGS % SPEEDS)).astype(np.float32)
    vx = speed * np.cos(heading)
    vy = speed * np.sin(heading)
    return np.stack([vx, vy]).astype(np.float32).reshape(2, SUB, LANE)


def corrections(s1, s2, s3, x1, x2):
    a = s2 * s3
    b = s1 * s3
    c = s1 * s2
    r1 = a * a
    r2 = b * b
    r3 = c * c
    mid = r1 + r3 + 6.0 * r2
    den_right = mid + (r3 + r3)
    den_left = mid + (r1 + r1)
    y1 = r1 * x1
    y2 = r3 * x2
    both = y1 + y2
    both = both + both
    right = (both + y2) / den_right
    left = (both + y1) / den_left
    return right, left


def smooth_outer(inner, outer_sq, inner_sq, product):
    return (2.5 * inner_sq - 2.75 * product) + outer_sq


def line_slopes(cells, eps):
    n = len(cells) - 6
    diff = [b - a for a, b in zip(cells[:-1], cells[1:])]
    second = [b - a for a, b in zip(diff[:-1], diff[1:])]
    third = [b - a for a, b in zip(second[:-1], second[1:])]
    fourth = [b - a for a, b in zip(third[:-1], third[1:])]
    sq = [e * e for e in second]
    sq_eps = [q + eps for q in sq]
    sq_big = [2.5 * q for q in sq]
    product = [a * b for a, b in zip(second[:-1], second[1:])]
    prod_outer = [2.75 * q for q in product]
    prod_inner = [1.25 * q for q in product]
    rights, lefts = [], []
    for k in range(n + 1):
        s1 = (sq_big[k + 1] - prod_outer[k]) + sq_eps[k]
        s2 = (sq[k + 1] - prod_inner[k + 1]) + sq_eps[k + 2]
        s3 = (sq_big[k + 2] - prod_outer[k + 2]) + sq_eps[k + 3]
        right, left = corrections(s1, s2, s3, fourth[k], fourth[k + 1])
        rights.append(right)
        lefts.append(left)
    sums, gaps = [], []
    for i in range(n):
        right, left = rights[i], lefts[i + 1]
        central = 6.0 * (diff[i + 2] + diff[i + 3]) - (second[i + 3] - second[i + 1])
        sums.append(central + (left - right))
        gaps.append((left + right) - fourth[i + 1])
    return sums, gaps


def edge_correction(g, eps):
    s = g * g + eps
    return (3.0 * eps * eps) * g / (7.0 * (s * s) + 3.0 * eps * eps)


def turn_slopes(cells, eps):
    d0, d1, d2 = (b - a for a, b in zip(cells[:-1], cells[1:]))
    e1 = d1 - d0
    e2 = d2 - d1
    sq1, sq2, p12 = e1 * e1, e2 * e2, e1 * e2
    big1, big2 = 2.5 * sq1, 2.5 * sq2
    one1, one2 = sq1 + eps, sq2 + eps
    x0, x1, x2, x3 = e1, e2 - (e1 + e1), e1 - (e2 + e2), e2
    outer = 2.75 * p12
    right_edge = edge_correction(e1, eps)
    left_edge = edge_correction(e2, eps)
    r0, l0 = corrections(eps, one1, (big1 - outer) + one2, x0, x1)
    r1, l1 = corrections(big1 + eps, (sq1 - 1.25 * p12) + one2, big2 + eps, x1, x2)
    r2, l2 = corrections((big2 - outer) + one1, one2, eps, x2, x3)
    rights, lefts = (right_edge, r0, r1, r2), (l0, l1, l2, left_edge)
    centrals = (
        12.0 * d0 - e1,
        6.0 * (d0 + d1) - e2,
        6.0 * (d1 + d2) + e1,
        12.0 * d2 + e2,
    )
    sums = [c + (le - ri) for c, le, ri in zip(centrals, lefts, rights)]
    gaps = [(le + ri) - x for x, le, ri in zip((x0, x1, x2, x3), lefts, rights)]
    return sums, gaps


def lane_corrections(em, e, ep, epp, eps):
    tm, t, tp = e - em, ep - e, epp - ep
    sq, sqp = e * e, ep * ep
    sqp_eps = sqp + eps
    s1 = e * (2.5 * e - 2.75 * em) + (em * em + eps)
    s2 = e * (e - 1.25 * ep) + sqp_eps
    s3 = ep * (2.5 * ep - 2.75 * epp) + (epp * epp + eps)
    x1 = t - tm
    right, left = corrections(s1, s2, s3, x1, tp - t)
    return right, left, x1


def heading_slopes(f, lane):
    place = lane % HEADINGS

    def moved(v, by):
        near = pltpu.roll(v, (-by) % LANE, 1)
        wrapped = pltpu.roll(v, (HEADINGS - by if by > 0 else -HEADINGS - by) % LANE, 1)
        inside = place < HEADINGS - by if by > 0 else place >= -by
        return jnp.where(inside, near, wrapped)

    d = moved(f, 1) - f
    dm = moved(d, -1)
    e = d - dm
    em, ep, epp = moved(e, -1), moved(e, 1), moved(e, 2)
    right, left, x1 = lane_corrections(em, e, ep, epp, EPS_HEADING)
    right = moved(right, -1)
    return 6.0 * (d + dm) - (ep - em) + (left - right), (left + right) - x1


def speed_slopes(pair, lane):
    first = lane < HEADINGS
    last = lane >= LANE - HEADINGS

    def up(vs):
        r0, r1 = (pltpu.roll(v, LANE - HEADINGS, 1) for v in vs)
        return jnp.where(last, r1, r0), jnp.where(last, r0, r1)

    def down(vs):
        r0, r1 = (pltpu.roll(v, HEADINGS, 1) for v in vs)
        return jnp.where(first, r1, r0), jnp.where(first, r0, r1)

    d = [b - a for a, b in zip(pair, up(pair))]
    dm = list(down(d))
    d[1] = jnp.where(last, dm[1], d[1])
    dm[0] = jnp.where(first, d[0], dm[0])
    e = [a - b for a, b in zip(d, dm)]
    em = down(e)
    ep = up(e)
    epp = list(up(ep))
    epp[1] = jnp.where(last, 0.0, epp[1])
    out = [lane_corrections(em[k], e[k], ep[k], epp[k], EPS_XY) for k in range(2)]
    rights = list(down((out[0][0], out[1][0])))
    rights[0] = jnp.where(first, edge_correction(ep[0], EPS_XY), rights[0])
    sums = [
        6.0 * (d[k] + dm[k]) - (ep[k] - em[k]) + (out[k][1] - rights[k]) for k in range(2)
    ]
    gaps = [(out[k][1] + rights[k]) - out[k][2] for k in range(2)]
    return sums, gaps


def kernel(
    gx_count,
    gy_count,
    u_hbm,
    dist_hbm,
    coord_hbm,
    out_ref,
    u_ref,
    dist_ref,
    coord_ref,
    frame,
    turned,
    flat,
    py,
    rates,
    alpha,
    peak,
    arsend,
    arrecv,
    load_sem,
    send_x_sem,
    recv_x_sem,
    send_y_sem,
    recv_y_sem,
    rate_send_sem,
    rate_recv_sem,
    rate_recv_x_sem,
    ar_send_sem,
    ar_recv_sem,
):
    gx = lax.axis_index("gx")
    gy = lax.axis_index("gy")

    loads = [
        pltpu.make_async_copy(src, dst, load_sem.at[k])
        for k, (src, dst) in enumerate(
            ((u_hbm, u_ref), (dist_hbm, dist_ref), (coord_hbm, coord_ref))
        )
    ]
    for load in loads:
        load.start()

    barrier = pltpu.get_barrier_semaphore()
    for count, axis in ((gx_count, 0), (gy_count, 1)):

        @pl.loop(0, count - 1)
        def _(i, count=count, axis=axis):
            k = i + count // 3 + 1
            k = jnp.where(k < count, k, k - count + 1)
            where = (lax.rem(gx + k, count), gy) if axis == 0 else (gx, lax.rem(gy + k, count))
            pl.semaphore_signal(barrier, inc=1, device_id=where, device_id_type=MESH)

    lane = lax.broadcasted_iota(jnp.int32, (SUB, LANE), 1)

    def cell(s, x, y):
        return (s * FX + x, pl.ds(y * SUB, SUB), slice(None))

    for load in loads:
        load.wait()

    for x in range(NX):
        for j in range(TILES):
            tile = u_ref[x, :, j * LANE : (j + 1) * LANE]
            turned[x, pl.ds(j * PITCH, NY), :] = SCALE * tile
    for x in range(NX):
        for y in range(NY):
            frame[cell(0, 3 + x, 3 + y)] = turned[x, pl.ds(y, SUB, stride=PITCH), :]

    def flat_pass():
        @pl.loop(0, NX)
        def _(x):
            tiles = [turned[x, pl.ds(j * PITCH, NY), :] for j in range(TILES)]
            parts = [None] * TILES
            for j in range(TILES):
                total, gap = heading_slopes(tiles[j], lane)
                rate = 0.1 * (j // 2 - (TURNS - 1) / 2.0)
                parts[j] = (turn_peak / (12.0 * step_heading)) * gap - (
                    rate / (12.0 * step_heading)
                ) * total
            for c in range(TURNS):
                sums, gaps = speed_slopes(tiles[2 * c : 2 * c + 2], lane)
                for k in range(2):
                    parts[2 * c + k] += (accel / (12.0 * step_xy)) * (gaps[k] - jnp.abs(sums[k]))
            for k in range(2):
                sums, gaps = turn_slopes(tiles[k::2], EPS_XY)
                for c in range(TURNS):
                    parts[2 * c + k] += (torque / (12.0 * step_xy)) * (gaps[c] - jnp.abs(sums[c]))
            for j in range(TILES):
                flat[x, pl.ds(j * PITCH, NY), :] = parts[j]

    sends = (gx < gx_count - 1, gx > 0, gy < gy_count - 1, gy > 0)
    receives = (gx > 0, gx < gx_count - 1, gy > 0, gy < gy_count - 1)

    def halo_x(s, way, y):
        row = s * FX
        turn = lax.rem(s, 2)
        at = pl.ds((3 + y) * SUB, SUB)
        return pltpu.make_async_remote_copy(
            src_ref=frame.at[pl.ds(row + (4 if way == 0 else 3), 3), at],
            dst_ref=frame.at[pl.ds(row + (0 if way == 0 else 3 + NX), 3), at],
            send_sem=send_x_sem.at[turn, way],
            recv_sem=recv_x_sem.at[turn, way, y],
            device_id=(gx + 1, gy) if way == 0 else (gx - 1, gy),
            device_id_type=MESH,
        )

    def halo_y(s, way):
        rows = pl.ds(s * FX + 3, NX)
        turn = lax.rem(s, 2)
        return pltpu.make_async_remote_copy(
            src_ref=frame.at[rows, pl.ds((NY if way == 0 else 3) * SUB, 3 * SUB)],
            dst_ref=frame.at[rows, pl.ds((0 if way == 0 else 3 + NY) * SUB, 3 * SUB)],
            send_sem=send_y_sem.at[turn, way],
            recv_sem=recv_y_sem.at[turn, way],
            device_id=(gx, gy + 1) if way == 0 else (gx, gy - 1),
            device_id_type=MESH,
        )

    def column(i):
        return jnp.where(i < 3, i, jnp.where(i < 6, i + 2, i - 3))

    def send_column(s, y):
        for way in range(2):

            @pl.when(sends[way])
            def _(way=way):
                halo_x(s, way, y).start()

    def send_rows(s, i):
        for way, last in ((1, 2), (0, 5)):

            @pl.when(jnp.logical_and(i == last, sends[2 + way]))
            def _(way=way):
                halo_y(s, way).start()

    def finish_sends(s):
        turn = lax.rem(s, 2)
        every = frame.at[pl.ds(0, 3), pl.ds(3 * SUB, NY * SUB)]
        for way in range(2):

            @pl.when(sends[way])
            def _(way=way):
                pltpu.make_async_remote_copy(
                    src_ref=every,
                    dst_ref=every,
                    send_sem=send_x_sem.at[turn, way],
                    recv_sem=recv_x_sem.at[turn, way, 0],
                    device_id=(gx, gy),
                    device_id_type=MESH,
                ).wait_send()

            @pl.when(sends[2 + way])
            def _(way=way):
                halo_y(s, way).wait_send()

    def rate_x(way, y):
        at = pl.ds((3 + y) * SUB, SUB)
        return pltpu.make_async_remote_copy(
            src_ref=rates.at[pl.ds(0, 3), pl.ds(4 if way == 0 else 3, 3), at],
            dst_ref=rates.at[pl.ds(0, 3), pl.ds(0 if way == 0 else 3 + NX, 3), at],
            send_sem=rate_send_sem.at[way],
            recv_sem=rate_recv_x_sem.at[way, y],
            device_id=(gx + 1, gy) if way == 0 else (gx - 1, gy),
            device_id_type=MESH,
        )

    def rate_y(way):
        rows = pl.ds(3, NX)
        return pltpu.make_async_remote_copy(
            src_ref=rates.at[pl.ds(0, 3), rows, pl.ds((NY if way == 0 else 3) * SUB, 3 * SUB)],
            dst_ref=rates.at[pl.ds(0, 3), rows, pl.ds((0 if way == 0 else 3 + NY) * SUB, 3 * SUB)],
            send_sem=rate_send_sem.at[2 + way],
            recv_sem=rate_recv_sem.at[way],
            device_id=(gx, gy + 1) if way == 0 else (gx, gy - 1),
            device_id_type=MESH,
        )

    def send_rates(y):
        for way in range(2):

            @pl.when(sends[way])
            def _(way=way):
                rate_x(way, y).start()

    def send_rate_rows():
        for way in range(2):

            @pl.when(sends[2 + way])
            def _(way=way):
                rate_y(way).start()

    def finish_rates():
        every = rates.at[pl.ds(0, 3), pl.ds(0, 3), pl.ds(3 * SUB, NY * SUB)]
        for way in range(2):

            @pl.when(sends[way])
            def _(way=way):
                pltpu.make_async_remote_copy(
                    src_ref=every,
                    dst_ref=every,
                    send_sem=rate_send_sem.at[way],
                    recv_sem=rate_recv_x_sem.at[way, 0],
                    device_id=(gx, gy),
                    device_id_type=MESH,
                ).wait_send()

            @pl.when(sends[2 + way])
            def _(way=way):
                rate_y(way).wait_send()

    def first_moved(s, x, y):
        at = pl.ds(y * SUB, SUB)
        rate = rates[0, x, at, :] + (alpha[0] * rates[1, x, at, :] + alpha[1] * rates[2, x, at, :])
        return frame[cell(s - 1, x, y)] + alpha[2] * rate

    def first_move(s, x, y):
        frame[cell(s, x, y)] = first_moved(s, x, y)

    def fill_ghosts(s):
        for low, outside in ((True, gx == 0), (False, gx == gx_count - 1)):

            @pl.when(outside)
            def _(low=low):
                end, inner, step = (3, 4, -1) if low else (2 + NX, 1 + NX, 1)

                @pl.loop(0, NY)
                def _(y):
                    edge = frame[cell(s, end, 3 + y)]
                    slope = edge - frame[cell(s, inner, 3 + y)]
                    for k in (1, 2, 3):
                        frame[cell(s, end + step * k, 3 + y)] = edge + float(k) * slope

        for low, outside in ((True, gy == 0), (False, gy == gy_count - 1)):

            @pl.when(outside)
            def _(low=low):
                end, inner, step = (3, 4, -1) if low else (2 + NY, 1 + NY, 1)

                @pl.loop(0, NX)
                def _(x):
                    edge = frame[cell(s, 3 + x, end)]
                    slope = edge - frame[cell(s, 3 + x, inner)]
                    for k in (1, 2, 3):
                        frame[cell(s, 3 + x, end + step * k)] = edge + float(k) * slope

    def second_pass(s, third):
        slot = jnp.where(third == 0, 2, 3)

        for way in range(2):

            @pl.when(jnp.logical_and(receives[2 + way], third != 1))
            def _(way=way):
                halo_y(s, way).wait_recv()

            @pl.when(jnp.logical_and(receives[2 + way], third == 1))
            def _(way=way):
                rate_y(way).wait_recv()

                @pl.loop(0, NX)
                def _(x):
                    for k in range(3):
                        first_move(s, 3 + x, k + (0 if way == 0 else 3 + NY))

        @pl.loop(0, NX)
        def _(x):
            sums, gaps = line_slopes([frame[cell(s, 3 + x, i)] for i in range(FY)], EPS_XY)
            for y in range(NY):
                py[x, pl.ds(y * SUB, SUB), :] = sums[y]
                rates[slot, 3 + x, pl.ds((3 + y) * SUB, SUB), :] = gaps[y]

    def first_slopes(s, y):
        sums, gaps = line_slopes([frame[cell(s, i, 3 + y)] for i in range(FX)], EPS_XY)
        vx = coord_ref[0]
        vy = coord_ref[1]
        top_x, top_y = peak[0], peak[1]
        moves = []
        for x in range(NX):
            at = (x, pl.ds(y * SUB, SUB), slice(None))
            bound = dist_ref[x, y]
            sx, sy = sums[x], py[at]
            square = sx * sx + sy * sy + RADIUS
            pull = bound * lax.rsqrt(square)
            top_x = jnp.maximum(top_x, jnp.abs(vx - pull * sx))
            top_y = jnp.maximum(top_y, jnp.abs(vy - pull * sy))
            moves.append(
                flat[x, pl.ds(y, SUB, stride=PITCH), :] + (1.0 / (12.0 * step_xy)) * ((pull * square) - (sx * vx + sy * vy))
            )
        peak[0] = top_x
        peak[1] = top_y
        return moves, gaps

    half = lane < LANE // 2

    def fold(v):
        for by in (4, 2, 1):
            v = jnp.maximum(v, pltpu.roll(v, by, 0))
        return jnp.maximum(v, pltpu.roll(v, LANE // 2, 1))

    def ar_copy(turn, phase, k):
        count = gy_count if phase == 1 else gx_count
        where = (gx, lax.rem(gy + k, count)) if phase == 1 else (lax.rem(gx + k, count), gy)
        return pltpu.make_async_remote_copy(
            src_ref=arsend.at[2 * turn + phase],
            dst_ref=arrecv.at[2 * turn + phase, k - 1],
            send_sem=ar_send_sem.at[2 * turn + phase],
            recv_sem=ar_recv_sem.at[2 * turn + phase],
            device_id=where,
            device_id_type=MESH,
        )

    def ar_start(turn, phase, row):
        arsend[2 * turn + phase] = row

        count = gy_count if phase == 1 else gx_count

        @pl.loop(0, count - 1)
        def _(i):
            k = i + count // 3 + 1
            ar_copy(turn, phase, jnp.where(k < count, k, k - count + 1)).start()

    def ar_finish(turn, phase):
        count = gy_count if phase == 1 else gx_count
        slot = 2 * turn + phase
        every = arrecv.at[slot, pl.ds(0, count - 1)]
        whole = pltpu.make_async_remote_copy(
            src_ref=every,
            dst_ref=every,
            send_sem=ar_send_sem.at[slot],
            recv_sem=ar_recv_sem.at[slot],
            device_id=(gx, gy),
            device_id_type=MESH,
        )
        whole.wait_send()
        whole.wait_recv()
        row = arsend[slot]
        for k in range(count - 1):
            row = jnp.maximum(row, arrecv[slot, k])
        return row

    def own_row():
        return jnp.where(half, fold(peak[0]), fold(peak[1]))[0:1]

    def set_alpha(row):
        row = jnp.broadcast_to(row, (SUB, LANE))
        ax = jnp.max(jnp.where(half, row, 0.0), axis=1, keepdims=True)
        ay = jnp.max(jnp.where(half, 0.0, row), axis=1, keepdims=True)
        ax = jnp.broadcast_to(ax, (SUB, LANE))
        ay = jnp.broadcast_to(ay, (SUB, LANE))
        total = ax / step_xy + ay / step_xy + turn_peak / step_heading
        alpha[0] = (1.0 / (12.0 * step_xy)) * ax
        alpha[1] = (1.0 / (12.0 * step_xy)) * ay
        alpha[2] = 0.75 / (total + accel / step_xy + torque / step_xy)

    peak[...] = jnp.zeros_like(peak)

    pl.semaphore_wait(barrier, gx_count + gy_count - 2)

    @pl.loop(0, NY)
    def _(i):
        send_column(0, column(i))
        send_rows(0, i)

    @pl.loop(0, 6)
    def _(s):
        third = lax.rem(s, 3)
        base = s - third

        flat_pass()
        fill_ghosts(s)
        second_pass(s, third)

        @pl.when(third == 0)
        def _():
            @pl.loop(0, NY)
            def _(i):
                y = column(i)
                for way in range(2):

                    @pl.when(receives[way])
                    def _(way=way):
                        halo_x(s, way, y).wait_recv()

                moves, gaps = first_slopes(s, y)
                for x in range(NX):
                    rates[0, 3 + x, pl.ds((3 + y) * SUB, SUB), :] = moves[x]
                    rates[1, 3 + x, pl.ds((3 + y) * SUB, SUB), :] = gaps[x]

                @pl.when(jnp.logical_and(s == 3, i < 3))
                def _():
                    send_rates(y)

            @pl.when(s == 0)
            def _():
                ar_start(0, 0, own_row())

                send_rate_rows()

                @pl.loop(0, NY)
                def _(i):
                    send_rates(column(i))

                ar_start(0, 1, ar_finish(0, 0))
                set_alpha(ar_finish(0, 1))
                peak[...] = jnp.zeros_like(peak)

            @pl.when(s == 3)
            def _():
                ar_start(1, 1, ar_finish(1, 0))

                send_rate_rows()

                @pl.loop(3, NY)
                def _(i):
                    send_rates(column(i))

                set_alpha(ar_finish(1, 1))

            @pl.loop(0, NY)
            def _(y):
                for x in range(NX):
                    following = first_moved(s + 1, 3 + x, 3 + y)
                    frame[cell(s + 1, 3 + x, 3 + y)] = following
                    turned[x, pl.ds(y, SUB, stride=PITCH), :] = following

            finish_sends(s)

        def advance(y, keep, take):
            moves, gaps = first_slopes(s, y)
            ax, ay, dt = alpha[0], alpha[1], alpha[2]
            for x in range(NX):
                gap_y = rates[3, 3 + x, pl.ds((3 + y) * SUB, SUB), :]
                rate = moves[x] + (ax * gaps[x] + ay * gap_y)
                moved = frame[cell(s, 3 + x, 3 + y)] + dt * rate
                following = keep * frame[cell(base, 3 + x, 3 + y)] + take * moved
                frame[cell(s + 1, 3 + x, 3 + y)] = following
                turned[x, pl.ds(y, SUB, stride=PITCH), :] = following

        @pl.when(third == 1)
        def _():
            @pl.loop(0, NY)
            def _(i):
                y = column(i)
                for way in range(2):

                    @pl.when(receives[way])
                    def _(way=way):
                        rate_x(way, y).wait_recv()

                for way in range(2):
                    for k in range(3):
                        x = k + (0 if way == 0 else 3 + NX)
                        frame[cell(s, x, 3 + y)] = jnp.where(
                            receives[way], first_moved(s, x, 3 + y), frame[cell(s, x, 3 + y)]
                        )
                advance(y, 0.75, 0.25)
                send_column(s + 1, y)
                send_rows(s + 1, i)

            finish_rates()

        @pl.when(third == 2)
        def _():
            @pl.loop(0, NY)
            def _(i):
                y = column(i)
                for way in range(2):

                    @pl.when(receives[way])
                    def _(way=way):
                        halo_x(s, way, y).wait_recv()

                advance(y, 1.0 / 3.0, 2.0 / 3.0)

            finish_sends(s)

        @pl.when(s == 2)
        def _():
            ar_start(1, 0, own_row())

            @pl.loop(0, NY)
            def _(i):
                send_column(s + 1, column(i))
                send_rows(s + 1, i)

    for x in range(NX):
        for j in range(TILES):
            tile = turned[x, pl.ds(j * PITCH, NY), :]
            out_ref[x, :, j * LANE : (j + 1) * LANE] = (1.0 / SCALE) * tile


def body(gx_count, gy_count, initial_value, disturbance):
    most = max(gx_count, gy_count)
    return pl.pallas_call(
        functools.partial(kernel, gx_count, gy_count),
        out_shape=pltpu.VMEM((NX, NY, LANES), jnp.float32),
        in_specs=[pl.BlockSpec(memory_space=pl.ANY)] * 3,
        out_specs=pl.BlockSpec(memory_space=pltpu.VMEM),
        scratch_shapes=[
            pltpu.VMEM((NX, NY, LANES), jnp.float32),
            pltpu.SMEM((NX, NY), jnp.float32),
            pltpu.VMEM((2, SUB, LANE), jnp.float32),
            pltpu.VMEM((7 * FX, FY * SUB, LANE), jnp.float32),
            pltpu.VMEM((NX, TILES * PITCH, LANE), jnp.float32),
            pltpu.VMEM((NX, TILES * PITCH, LANE), jnp.float32),
            pltpu.VMEM((NX, NY * SUB, LANE), jnp.float32),
            pltpu.VMEM((4, FX, FY * SUB, LANE), jnp.float32),
            pltpu.VMEM((3, SUB, LANE), jnp.float32),
            pltpu.VMEM((2, SUB, LANE), jnp.float32),
            pltpu.VMEM((4, 1, LANE), jnp.float32),
            pltpu.VMEM((4, most - 1, 1, LANE), jnp.float32),
            pltpu.SemaphoreType.DMA((3,)),
            pltpu.SemaphoreType.DMA((2, 2)),
            pltpu.SemaphoreType.DMA((2, 2, NY)),
            pltpu.SemaphoreType.DMA((2, 2)),
            pltpu.SemaphoreType.DMA((2, 2)),
            pltpu.SemaphoreType.DMA((4,)),
            pltpu.SemaphoreType.DMA((2,)),
            pltpu.SemaphoreType.DMA((2, NY)),
            pltpu.SemaphoreType.DMA((4,)),
            pltpu.SemaphoreType.DMA((4,)),
        ],
        compiler_params=pltpu.CompilerParams(collective_id=0, has_side_effects=True),
    )(initial_value, disturbance, jnp.asarray(coordinate_tables()))


def solution(mesh):
    placed = (P("gx", "gy", None), P("gx", "gy"))
    return jax.shard_map(
        functools.partial(body, mesh.shape["gx"], mesh.shape["gy"]),
        mesh=mesh,
        in_specs=placed,
        out_specs=P("gx", "gy", None),
        check_vma=False,
    )
```

```python
import functools
import math

import jax
import jax.numpy as jnp
import numpy as np
from jax import lax
from jax.experimental import pallas as pl
from jax.experimental.pallas import tpu as pltpu
from jax.sharding import PartitionSpec as P

HEADINGS = 16
SPEEDS = 16
TURNS = 4
LANES = HEADINGS * SPEEDS * TURNS

NX = 4
NY = 8
SUB = 8
LANE = 128
TILES = LANES // LANE
PITCH = NY + 1
FX = NX + 6
FY = NY + 6

SCALE = 4.0
step_xy = 0.1
step_heading = 2.0 * math.pi / HEADINGS
accel = 0.5
torque = 0.3
turn_peak = 0.1 * (TURNS - 1) / 2.0
EPS_XY = 0.75e-6 * (SCALE * step_xy) ** 2
EPS_HEADING = 0.75e-6 * (SCALE * step_heading) ** 2
RADIUS = 0.01 * (SCALE * 12.0 * step_xy) ** 2

MESH = pl.DeviceIdType.MESH


def coordinate_tables():
    lanes = np.arange(LANES)
    heading = (-math.pi + ((lanes % HEADINGS) + 0.5) * step_heading).astype(np.float32)
    speed = (1.0 + 0.1 * (lanes // HEADINGS % SPEEDS)).astype(np.float32)
    vx = speed * np.cos(heading)
    vy = speed * np.sin(heading)
    return np.stack([vx, vy]).astype(np.float32).reshape(2, SUB, LANE)


def corrections(s1, s2, s3, x1, x2):
    a = s2 * s3
    b = s1 * s3
    c = s1 * s2
    r1 = a * a
    r2 = b * b
    r3 = c * c
    mid = r1 + r3 + 6.0 * r2
    den_right = mid + (r3 + r3)
    den_left = mid + (r1 + r1)
    y1 = r1 * x1
    y2 = r3 * x2
    both = y1 + y2
    both = both + both
    right = (both + y2) / den_right
    left = (both + y1) / den_left
    return right, left


def smooth_outer(inner, outer_sq, inner_sq, product):
    return (2.5 * inner_sq - 2.75 * product) + outer_sq


def line_slopes(cells, eps):
    n = len(cells) - 6
    diff = [b - a for a, b in zip(cells[:-1], cells[1:])]
    second = [b - a for a, b in zip(diff[:-1], diff[1:])]
    third = [b - a for a, b in zip(second[:-1], second[1:])]
    fourth = [b - a for a, b in zip(third[:-1], third[1:])]
    sq = [e * e for e in second]
    sq_eps = [q + eps for q in sq]
    sq_big = [2.5 * q for q in sq]
    product = [a * b for a, b in zip(second[:-1], second[1:])]
    prod_outer = [2.75 * q for q in product]
    prod_inner = [1.25 * q for q in product]
    rights, lefts = [], []
    for k in range(n + 1):
        s1 = (sq_big[k + 1] - prod_outer[k]) + sq_eps[k]
        s2 = (sq[k + 1] - prod_inner[k + 1]) + sq_eps[k + 2]
        s3 = (sq_big[k + 2] - prod_outer[k + 2]) + sq_eps[k + 3]
        right, left = corrections(s1, s2, s3, fourth[k], fourth[k + 1])
        rights.append(right)
        lefts.append(left)
    sums, gaps = [], []
    for i in range(n):
        right, left = rights[i], lefts[i + 1]
        central = 6.0 * (diff[i + 2] + diff[i + 3]) - (second[i + 3] - second[i + 1])
        sums.append(central + (left - right))
        gaps.append((left + right) - fourth[i + 1])
    return sums, gaps


def edge_correction(g, eps):
    s = g * g + eps
    return (3.0 * eps * eps) * g / (7.0 * (s * s) + 3.0 * eps * eps)


def turn_slopes(cells, eps):
    d0, d1, d2 = (b - a for a, b in zip(cells[:-1], cells[1:]))
    e1 = d1 - d0
    e2 = d2 - d1
    sq1, sq2, p12 = e1 * e1, e2 * e2, e1 * e2
    big1, big2 = 2.5 * sq1, 2.5 * sq2
    one1, one2 = sq1 + eps, sq2 + eps
    x0, x1, x2, x3 = e1, e2 - (e1 + e1), e1 - (e2 + e2), e2
    outer = 2.75 * p12
    right_edge = edge_correction(e1, eps)
    left_edge = edge_correction(e2, eps)
    r0, l0 = corrections(eps, one1, (big1 - outer) + one2, x0, x1)
    r1, l1 = corrections(big1 + eps, (sq1 - 1.25 * p12) + one2, big2 + eps, x1, x2)
    r2, l2 = corrections((big2 - outer) + one1, one2, eps, x2, x3)
    rights, lefts = (right_edge, r0, r1, r2), (l0, l1, l2, left_edge)
    centrals = (
        12.0 * d0 - e1,
        6.0 * (d0 + d1) - e2,
        6.0 * (d1 + d2) + e1,
        12.0 * d2 + e2,
    )
    sums = [c + (le - ri) for c, le, ri in zip(centrals, lefts, rights)]
    gaps = [(le + ri) - x for x, le, ri in zip((x0, x1, x2, x3), lefts, rights)]
    return sums, gaps


def lane_corrections(em, e, ep, epp, eps):
    tm, t, tp = e - em, ep - e, epp - ep
    sq, sqp = e * e, ep * ep
    sqp_eps = sqp + eps
    s1 = e * (2.5 * e - 2.75 * em) + (em * em + eps)
    s2 = e * (e - 1.25 * ep) + sqp_eps
    s3 = ep * (2.5 * ep - 2.75 * epp) + (epp * epp + eps)
    x1 = t - tm
    right, left = corrections(s1, s2, s3, x1, tp - t)
    return right, left, x1


def heading_slopes(f, lane):
    place = lane % HEADINGS

    def moved(v, by):
        near = pltpu.roll(v, (-by) % LANE, 1)
        wrapped = pltpu.roll(v, (HEADINGS - by if by > 0 else -HEADINGS - by) % LANE, 1)
        inside = place < HEADINGS - by if by > 0 else place >= -by
        return jnp.where(inside, near, wrapped)

    d = moved(f, 1) - f
    dm = moved(d, -1)
    e = d - dm
    em, ep, epp = moved(e, -1), moved(e, 1), moved(e, 2)
    right, left, x1 = lane_corrections(em, e, ep, epp, EPS_HEADING)
    right = moved(right, -1)
    return 6.0 * (d + dm) - (ep - em) + (left - right), (left + right) - x1


def speed_slopes(pair, lane):
    first = lane < HEADINGS
    last = lane >= LANE - HEADINGS

    def up(vs):
        r0, r1 = (pltpu.roll(v, LANE - HEADINGS, 1) for v in vs)
        return jnp.where(last, r1, r0), jnp.where(last, r0, r1)

    def down(vs):
        r0, r1 = (pltpu.roll(v, HEADINGS, 1) for v in vs)
        return jnp.where(first, r1, r0), jnp.where(first, r0, r1)

    d = [b - a for a, b in zip(pair, up(pair))]
    dm = list(down(d))
    d[1] = jnp.where(last, dm[1], d[1])
    dm[0] = jnp.where(first, d[0], dm[0])
    e = [a - b for a, b in zip(d, dm)]
    em = down(e)
    ep = up(e)
    epp = list(up(ep))
    epp[1] = jnp.where(last, 0.0, epp[1])
    out = [lane_corrections(em[k], e[k], ep[k], epp[k], EPS_XY) for k in range(2)]
    rights = list(down((out[0][0], out[1][0])))
    rights[0] = jnp.where(first, edge_correction(ep[0], EPS_XY), rights[0])
    sums = [
        6.0 * (d[k] + dm[k]) - (ep[k] - em[k]) + (out[k][1] - rights[k]) for k in range(2)
    ]
    gaps = [(out[k][1] + rights[k]) - out[k][2] for k in range(2)]
    return sums, gaps


def kernel(
    gx_count,
    gy_count,
    u_hbm,
    dist_hbm,
    coord_hbm,
    out_ref,
    u_ref,
    dist_ref,
    coord_ref,
    frame,
    turned,
    flat,
    py,
    rates,
    alpha,
    peak,
    arsend,
    arrecv,
    load_sem,
    send_x_sem,
    recv_x_sem,
    send_y_sem,
    recv_y_sem,
    rate_send_sem,
    rate_recv_sem,
    rate_recv_x_sem,
    ar_send_sem,
    ar_recv_sem,
):
    gx = lax.axis_index("gx")
    gy = lax.axis_index("gy")

    loads = [
        pltpu.make_async_copy(src, dst, load_sem.at[k])
        for k, (src, dst) in enumerate(
            ((u_hbm, u_ref), (dist_hbm, dist_ref), (coord_hbm, coord_ref))
        )
    ]
    for load in loads:
        load.start()

    barrier = pltpu.get_barrier_semaphore()
    for count, axis in ((gx_count, 0), (gy_count, 1)):

        @pl.loop(0, count - 1)
        def _(i, count=count, axis=axis):
            k = i + count // 3 + 1
            k = jnp.where(k < count, k, k - count + 1)
            where = (lax.rem(gx + k, count), gy) if axis == 0 else (gx, lax.rem(gy + k, count))
            pl.semaphore_signal(barrier, inc=1, device_id=where, device_id_type=MESH)

    lane = lax.broadcasted_iota(jnp.int32, (SUB, LANE), 1)

    def cell(s, x, y):
        return (s * FX + x, pl.ds(y * SUB, SUB), slice(None))

    for load in loads:
        load.wait()

    for x in range(NX):
        for j in range(TILES):
            tile = u_ref[x, :, j * LANE : (j + 1) * LANE]
            turned[x, pl.ds(j * PITCH, NY), :] = SCALE * tile
    for x in range(NX):
        for y in range(NY):
            frame[cell(0, 3 + x, 3 + y)] = turned[x, pl.ds(y, SUB, stride=PITCH), :]

    def flat_pass():
        @pl.loop(0, NX)
        def _(x):
            tiles = [turned[x, pl.ds(j * PITCH, NY), :] for j in range(TILES)]
            parts = [None] * TILES
            for j in range(TILES):
                total, gap = heading_slopes(tiles[j], lane)
                rate = 0.1 * (j // 2 - (TURNS - 1) / 2.0)
                parts[j] = (turn_peak / (12.0 * step_heading)) * gap - (
                    rate / (12.0 * step_heading)
                ) * total
            for c in range(TURNS):
                sums, gaps = speed_slopes(tiles[2 * c : 2 * c + 2], lane)
                for k in range(2):
                    parts[2 * c + k] += (accel / (12.0 * step_xy)) * (gaps[k] - jnp.abs(sums[k]))
            for k in range(2):
                sums, gaps = turn_slopes(tiles[k::2], EPS_XY)
                for c in range(TURNS):
                    parts[2 * c + k] += (torque / (12.0 * step_xy)) * (gaps[c] - jnp.abs(sums[c]))
            for j in range(TILES):
                flat[x, pl.ds(j * PITCH, NY), :] = parts[j]

    sends = (gx < gx_count - 1, gx > 0, gy < gy_count - 1, gy > 0)
    receives = (gx > 0, gx < gx_count - 1, gy > 0, gy < gy_count - 1)

    def halo_x(s, way, y):
        row = s * FX
        turn = lax.rem(s, 2)
        at = pl.ds((3 + y) * SUB, SUB)
        return pltpu.make_async_remote_copy(
            src_ref=frame.at[pl.ds(row + (4 if way == 0 else 3), 3), at],
            dst_ref=frame.at[pl.ds(row + (0 if way == 0 else 3 + NX), 3), at],
            send_sem=send_x_sem.at[turn, way],
            recv_sem=recv_x_sem.at[turn, way, y],
            device_id=(gx + 1, gy) if way == 0 else (gx - 1, gy),
            device_id_type=MESH,
        )

    def halo_y(s, way):
        rows = pl.ds(s * FX + 3, NX)
        turn = lax.rem(s, 2)
        return pltpu.make_async_remote_copy(
            src_ref=frame.at[rows, pl.ds((NY if way == 0 else 3) * SUB, 3 * SUB)],
            dst_ref=frame.at[rows, pl.ds((0 if way == 0 else 3 + NY) * SUB, 3 * SUB)],
            send_sem=send_y_sem.at[turn, way],
            recv_sem=recv_y_sem.at[turn, way],
            device_id=(gx, gy + 1) if way == 0 else (gx, gy - 1),
            device_id_type=MESH,
        )

    def column(i):
        return jnp.where(i < 3, i, jnp.where(i < 6, i + 2, i - 3))

    def send_column(s, y):
        for way in range(2):

            @pl.when(sends[way])
            def _(way=way):
                halo_x(s, way, y).start()

    def send_rows(s, i):
        for way, last in ((1, 2), (0, 5)):

            @pl.when(jnp.logical_and(i == last, sends[2 + way]))
            def _(way=way):
                halo_y(s, way).start()

    def finish_sends(s):
        turn = lax.rem(s, 2)
        every = frame.at[pl.ds(0, 3), pl.ds(3 * SUB, NY * SUB)]
        for way in range(2):

            @pl.when(sends[way])
            def _(way=way):
                pltpu.make_async_remote_copy(
                    src_ref=every,
                    dst_ref=every,
                    send_sem=send_x_sem.at[turn, way],
                    recv_sem=recv_x_sem.at[turn, way, 0],
                    device_id=(gx, gy),
                    device_id_type=MESH,
                ).wait_send()

            @pl.when(sends[2 + way])
            def _(way=way):
                halo_y(s, way).wait_send()

    def rate_x(way, y):
        at = pl.ds((3 + y) * SUB, SUB)
        return pltpu.make_async_remote_copy(
            src_ref=rates.at[pl.ds(0, 3), pl.ds(4 if way == 0 else 3, 3), at],
            dst_ref=rates.at[pl.ds(0, 3), pl.ds(0 if way == 0 else 3 + NX, 3), at],
            send_sem=rate_send_sem.at[way],
            recv_sem=rate_recv_x_sem.at[way, y],
            device_id=(gx + 1, gy) if way == 0 else (gx - 1, gy),
            device_id_type=MESH,
        )

    def rate_y(way):
        rows = pl.ds(3, NX)
        return pltpu.make_async_remote_copy(
            src_ref=rates.at[pl.ds(0, 3), rows, pl.ds((NY if way == 0 else 3) * SUB, 3 * SUB)],
            dst_ref=rates.at[pl.ds(0, 3), rows, pl.ds((0 if way == 0 else 3 + NY) * SUB, 3 * SUB)],
            send_sem=rate_send_sem.at[2 + way],
            recv_sem=rate_recv_sem.at[way],
            device_id=(gx, gy + 1) if way == 0 else (gx, gy - 1),
            device_id_type=MESH,
        )

    def send_rates(y):
        for way in range(2):

            @pl.when(sends[way])
            def _(way=way):
                rate_x(way, y).start()

    def send_rate_rows():
        for way in range(2):

            @pl.when(sends[2 + way])
            def _(way=way):
                rate_y(way).start()

    def finish_rates():
        every = rates.at[pl.ds(0, 3), pl.ds(0, 3), pl.ds(3 * SUB, NY * SUB)]
        for way in range(2):

            @pl.when(sends[way])
            def _(way=way):
                pltpu.make_async_remote_copy(
                    src_ref=every,
                    dst_ref=every,
                    send_sem=rate_send_sem.at[way],
                    recv_sem=rate_recv_x_sem.at[way, 0],
                    device_id=(gx, gy),
                    device_id_type=MESH,
                ).wait_send()

            @pl.when(sends[2 + way])
            def _(way=way):
                rate_y(way).wait_send()

    def first_moved(s, x, y):
        at = pl.ds(y * SUB, SUB)
        rate = rates[0, x, at, :] + (alpha[0] * rates[1, x, at, :] + alpha[1] * rates[2, x, at, :])
        return frame[cell(s - 1, x, y)] + alpha[2] * rate

    def first_move(s, x, y):
        frame[cell(s, x, y)] = first_moved(s, x, y)

    def fill_ghosts(s):
        for low, outside in ((True, gx == 0), (False, gx == gx_count - 1)):

            @pl.when(outside)
            def _(low=low):
                end, inner, step = (3, 4, -1) if low else (2 + NX, 1 + NX, 1)

                @pl.loop(0, NY)
                def _(y):
                    edge = frame[cell(s, end, 3 + y)]
                    slope = edge - frame[cell(s, inner, 3 + y)]
                    for k in (1, 2, 3):
                        frame[cell(s, end + step * k, 3 + y)] = edge + float(k) * slope

        for low, outside in ((True, gy == 0), (False, gy == gy_count - 1)):

            @pl.when(outside)
            def _(low=low):
                end, inner, step = (3, 4, -1) if low else (2 + NY, 1 + NY, 1)

                @pl.loop(0, NX)
                def _(x):
                    edge = frame[cell(s, 3 + x, end)]
                    slope = edge - frame[cell(s, 3 + x, inner)]
                    for k in (1, 2, 3):
                        frame[cell(s, 3 + x, end + step * k)] = edge + float(k) * slope

    def second_pass(s, third):
        slot = jnp.where(third == 0, 2, 3)

        for way in range(2):

            @pl.when(jnp.logical_and(receives[2 + way], third != 1))
            def _(way=way):
                halo_y(s, way).wait_recv()

            @pl.when(jnp.logical_and(receives[2 + way], third == 1))
            def _(way=way):
                rate_y(way).wait_recv()

                @pl.loop(0, NX)
                def _(x):
                    for k in range(3):
                        first_move(s, 3 + x, k + (0 if way == 0 else 3 + NY))

        @pl.loop(0, NX)
        def _(x):
            sums, gaps = line_slopes([frame[cell(s, 3 + x, i)] for i in range(FY)], EPS_XY)
            for y in range(NY):
                py[x, pl.ds(y * SUB, SUB), :] = sums[y]
                rates[slot, 3 + x, pl.ds((3 + y) * SUB, SUB), :] = gaps[y]

    def first_slopes(s, y):
        sums, gaps = line_slopes([frame[cell(s, i, 3 + y)] for i in range(FX)], EPS_XY)
        vx = coord_ref[0]
        vy = coord_ref[1]
        top_x, top_y = peak[0], peak[1]
        moves = []
        for x in range(NX):
            at = (x, pl.ds(y * SUB, SUB), slice(None))
            bound = dist_ref[x, y]
            sx, sy = sums[x], py[at]
            square = sx * sx + sy * sy + RADIUS
            pull = bound * lax.rsqrt(square)
            top_x = jnp.maximum(top_x, jnp.abs(vx - pull * sx))
            top_y = jnp.maximum(top_y, jnp.abs(vy - pull * sy))
            moves.append(
                flat[x, pl.ds(y, SUB, stride=PITCH), :] + (1.0 / (12.0 * step_xy)) * ((pull * square) - (sx * vx + sy * vy))
            )
        peak[0] = top_x
        peak[1] = top_y
        return moves, gaps

    half = lane < LANE // 2

    def fold(v):
        for by in (4, 2, 1):
            v = jnp.maximum(v, pltpu.roll(v, by, 0))
        return jnp.maximum(v, pltpu.roll(v, LANE // 2, 1))

    def ar_copy(turn, phase, k):
        count = gy_count if phase == 1 else gx_count
        where = (gx, lax.rem(gy + k, count)) if phase == 1 else (lax.rem(gx + k, count), gy)
        return pltpu.make_async_remote_copy(
            src_ref=arsend.at[2 * turn + phase],
            dst_ref=arrecv.at[2 * turn + phase, k - 1],
            send_sem=ar_send_sem.at[2 * turn + phase],
            recv_sem=ar_recv_sem.at[2 * turn + phase],
            device_id=where,
            device_id_type=MESH,
        )

    def ar_start(turn, phase, row):
        arsend[2 * turn + phase] = row

        count = gy_count if phase == 1 else gx_count

        @pl.loop(0, count - 1)
        def _(i):
            k = i + count // 3 + 1
            ar_copy(turn, phase, jnp.where(k < count, k, k - count + 1)).start()

    def ar_finish(turn, phase):
        count = gy_count if phase == 1 else gx_count
        slot = 2 * turn + phase
        every = arrecv.at[slot, pl.ds(0, count - 1)]
        whole = pltpu.make_async_remote_copy(
            src_ref=every,
            dst_ref=every,
            send_sem=ar_send_sem.at[slot],
            recv_sem=ar_recv_sem.at[slot],
            device_id=(gx, gy),
            device_id_type=MESH,
        )
        whole.wait_send()
        whole.wait_recv()
        row = arsend[slot]
        for k in range(count - 1):
            row = jnp.maximum(row, arrecv[slot, k])
        return row

    def own_row():
        return jnp.where(half, fold(peak[0]), fold(peak[1]))[0:1]

    def set_alpha(row):
        row = jnp.broadcast_to(row, (SUB, LANE))
        ax = jnp.max(jnp.where(half, row, 0.0), axis=1, keepdims=True)
        ay = jnp.max(jnp.where(half, 0.0, row), axis=1, keepdims=True)
        ax = jnp.broadcast_to(ax, (SUB, LANE))
        ay = jnp.broadcast_to(ay, (SUB, LANE))
        total = ax / step_xy + ay / step_xy + turn_peak / step_heading
        alpha[0] = (1.0 / (12.0 * step_xy)) * ax
        alpha[1] = (1.0 / (12.0 * step_xy)) * ay
        alpha[2] = 0.75 / (total + accel / step_xy + torque / step_xy)

    peak[...] = jnp.zeros_like(peak)

    pl.semaphore_wait(barrier, gx_count + gy_count - 2)

    @pl.loop(0, NY)
    def _(i):
        send_column(0, column(i))
        send_rows(0, i)

    @pl.loop(0, 6)
    def _(s):
        third = lax.rem(s, 3)
        base = s - third

        flat_pass()
        fill_ghosts(s)
        second_pass(s, third)

        @pl.when(third == 0)
        def _():
            @pl.loop(0, NY)
            def _(i):
                y = column(i)
                for way in range(2):

                    @pl.when(receives[way])
                    def _(way=way):
                        halo_x(s, way, y).wait_recv()

                moves, gaps = first_slopes(s, y)
                for x in range(NX):
                    rates[0, 3 + x, pl.ds((3 + y) * SUB, SUB), :] = moves[x]
                    rates[1, 3 + x, pl.ds((3 + y) * SUB, SUB), :] = gaps[x]

                @pl.when(jnp.logical_and(s == 3, i < 3))
                def _():
                    send_rates(y)

            @pl.when(s == 0)
            def _():
                ar_start(0, 0, own_row())

                send_rate_rows()

                @pl.loop(0, NY)
                def _(i):
                    send_rates(column(i))

                ar_start(0, 1, ar_finish(0, 0))
                set_alpha(ar_finish(0, 1))
                peak[...] = jnp.zeros_like(peak)

            @pl.when(s == 3)
            def _():
                ar_start(1, 1, ar_finish(1, 0))

                send_rate_rows()

                @pl.loop(3, NY)
                def _(i):
                    send_rates(column(i))

                set_alpha(ar_finish(1, 1))

            @pl.loop(0, NY)
            def _(y):
                for x in range(NX):
                    following = first_moved(s + 1, 3 + x, 3 + y)
                    frame[cell(s + 1, 3 + x, 3 + y)] = following
                    turned[x, pl.ds(y, SUB, stride=PITCH), :] = following

            finish_sends(s)

        def advance(y, keep, take):
            moves, gaps = first_slopes(s, y)
            ax, ay, dt = alpha[0], alpha[1], alpha[2]
            for x in range(NX):
                gap_y = rates[3, 3 + x, pl.ds((3 + y) * SUB, SUB), :]
                rate = moves[x] + (ax * gaps[x] + ay * gap_y)
                moved = frame[cell(s, 3 + x, 3 + y)] + dt * rate
                following = keep * frame[cell(base, 3 + x, 3 + y)] + take * moved
                frame[cell(s + 1, 3 + x, 3 + y)] = following
                turned[x, pl.ds(y, SUB, stride=PITCH), :] = following

        @pl.when(third == 1)
        def _():
            @pl.loop(0, NY)
            def _(i):
                y = column(i)
                for way in range(2):

                    @pl.when(receives[way])
                    def _(way=way):
                        rate_x(way, y).wait_recv()

                for way in range(2):
                    for k in range(3):
                        x = k + (0 if way == 0 else 3 + NX)
                        frame[cell(s, x, 3 + y)] = jnp.where(
                            receives[way], first_moved(s, x, 3 + y), frame[cell(s, x, 3 + y)]
                        )
                advance(y, 0.75, 0.25)
                send_column(s + 1, y)
                send_rows(s + 1, i)

            finish_rates()

        @pl.when(third == 2)
        def _():
            @pl.loop(0, NY)
            def _(i):
                y = column(i)
                for way in range(2):

                    @pl.when(receives[way])
                    def _(way=way):
                        halo_x(s, way, y).wait_recv()

                advance(y, 1.0 / 3.0, 2.0 / 3.0)

                @pl.when(jnp.logical_and(s == 2, i < 4))
                def _():
                    send_column(s + 1, y)

            finish_sends(s)

        @pl.when(s == 2)
        def _():
            ar_start(1, 0, own_row())

            @pl.loop(0, NY)
            def _(i):
                send_rows(s + 1, i)

            @pl.loop(4, NY)
            def _(i):
                send_column(s + 1, column(i))

    for x in range(NX):
        for j in range(TILES):
            tile = turned[x, pl.ds(j * PITCH, NY), :]
            out_ref[x, :, j * LANE : (j + 1) * LANE] = (1.0 / SCALE) * tile


def body(gx_count, gy_count, initial_value, disturbance):
    most = max(gx_count, gy_count)
    return pl.pallas_call(
        functools.partial(kernel, gx_count, gy_count),
        out_shape=pltpu.VMEM((NX, NY, LANES), jnp.float32),
        in_specs=[pl.BlockSpec(memory_space=pl.ANY)] * 3,
        out_specs=pl.BlockSpec(memory_space=pltpu.VMEM),
        scratch_shapes=[
            pltpu.VMEM((NX, NY, LANES), jnp.float32),
            pltpu.SMEM((NX, NY), jnp.float32),
            pltpu.VMEM((2, SUB, LANE), jnp.float32),
            pltpu.VMEM((7 * FX, FY * SUB, LANE), jnp.float32),
            pltpu.VMEM((NX, (TILES + 1) * PITCH - 1, LANE), jnp.float32),
            pltpu.VMEM((NX, (TILES + 1) * PITCH - 1, LANE), jnp.float32),
            pltpu.VMEM((NX, NY * SUB, LANE), jnp.float32),
            pltpu.VMEM((4, FX, FY * SUB, LANE), jnp.float32),
            pltpu.VMEM((3, SUB, LANE), jnp.float32),
            pltpu.VMEM((2, SUB, LANE), jnp.float32),
            pltpu.VMEM((4, 1, LANE), jnp.float32),
            pltpu.VMEM((4, most - 1, 1, LANE), jnp.float32),
            pltpu.SemaphoreType.DMA((3,)),
            pltpu.SemaphoreType.DMA((2, 2)),
            pltpu.SemaphoreType.DMA((2, 2, NY)),
            pltpu.SemaphoreType.DMA((2, 2)),
            pltpu.SemaphoreType.DMA((2, 2)),
            pltpu.SemaphoreType.DMA((4,)),
            pltpu.SemaphoreType.DMA((2,)),
            pltpu.SemaphoreType.DMA((2, NY)),
            pltpu.SemaphoreType.DMA((4,)),
            pltpu.SemaphoreType.DMA((4,)),
        ],
        compiler_params=pltpu.CompilerParams(collective_id=0, has_side_effects=True),
    )(initial_value, disturbance, jnp.asarray(coordinate_tables()))


def solution(mesh):
    placed = (P("gx", "gy", None), P("gx", "gy"))
    return jax.shard_map(
        functools.partial(body, mesh.shape["gx"], mesh.shape["gy"]),
        mesh=mesh,
        in_specs=placed,
        out_specs=P("gx", "gy", None),
        check_vma=False,
    )
```
